32 devices in a mesh: px: 4 (over x, core), py: 8 (over z, y).
Axes of the slice: x: 2, y: 2, z: 4, core: 2. Of those that a mesh axis runs over, the one named last changes fastest.
Arguments:
- displacement: float32 [3, 131072], P(None, ('px', 'py')), may hold values from -6 to 6
- disp_prev: float32 [3, 131072], P(None, ('px', 'py')), may hold values from -6 to 6
- nodal_load: float32 [3, 131072], P(None, ('px', 'py')), may hold values from -6 to 6
- nodal_mass: float32 [131072], P(('px', 'py')), may hold values from 1 to 4
- modulus: float32 [16384], P(('px', 'py')), may hold values from 1 to 10
- stiffness: float32 [81, 81], replicated
- connectivity: int32 [27, 16384], P(None, ('px', 'py')), may hold values from 0 to 4607, as said below
- ghost_send: int32 [2, 8192], P(None, ('px', 'py')), may hold values from 0 to 4095
- contact_node: int32 [65536], P(('px', 'py')), may hold values from 0 to 4095
- contact_owner: int32 [65536], P(('px', 'py')), may hold values from 0 to 31, as said below
- pair_ids: int32 [2, 32768], P(None, ('px', 'py')), may hold values from 0 to 4095
- gap_start: float32 [3, 32768], P(None, ('px', 'py')), may hold values from -3 to 3
- penalty: float32 [32768], P(('px', 'py')), may hold values from 0.5 to 2
- friction: float32 [32768], P(('px', 'py')), may hold values from 0.2 to 0.6
- slip_state: int32 [3, 32768], P(None, ('px', 'py')), may hold values 0 or 1
Outputs:
- new_displacement: float32 [3, 131072], P(None, ('px', 'py'))
- acceleration: float32 [3, 131072], P(None, ('px', 'py'))
The draws below stay inside these ranges and needn't reach their ends.
Inputs may be any that keep to these rules, and one draw needn't show every extreme that they name: `connectivity`: of each device's 512 elements, the first 384 name only the device's own nodes, indices below 4096; the others name own and ghost nodes. `contact_owner`: among the 2048 contact nodes of one device at most 128 name the same owner; one owner is named by exactly 128 nodes of every device.
All inputs are finite; a program needn't handle non-finite values. No bound on the sum of `slip_state` on one device may be relied on, other than what follows from the above.
Results may differ from the reference program's by a relative error of at most 0.0003.
Values sent between devices are 32-bit elements; how exact they have to be, the bound alone decides.
A program may use at most 64 MiB of HBM per device.

```python
import math
import jax
import jax.numpy as jnp
from jax import lax

ELNODE = 27
ELDOF = 81
STEPS = 3
NODE_DEV = 4096
NE_DEV = 512
HB = 256
CN_DEV = 2048
PAIRS_PER_OWNER = 1024
NE_IN = 384
OWNER_TOTAL = 32
CAP = 128
NODES = 131072
ELEMS = 16384
GHOSTS = 8192
CONTACT = 65536
PAIRS = 32768


def draw_stiffness(key, part):
    key_coupling, key_diagonal = jax.random.split(key)
    random_part = jax.random.uniform(key_coupling, (ELDOF, ELDOF), jnp.float32, -1.0, 1.0)
    diagonal = jax.random.uniform(key_diagonal, (ELDOF,), jnp.float32, 1.2, 1.6)
    coupling = 0.06 * (random_part + random_part.T)
    identity = jnp.eye(ELDOF, dtype=jnp.float32)
    return 0.05 * (coupling * (1.0 - identity) + jnp.diag(diagonal))


def draw_connectivity(key, part):
    key_any, key_own = jax.random.split(key)
    anywhere = jax.random.randint(key_any, (ELNODE, OWNER_TOTAL, NE_DEV), 0, NODE_DEV + 2 * HB)
    own_only = jax.random.randint(key_own, (ELNODE, OWNER_TOTAL, NE_DEV), 0, NODE_DEV)
    column = jnp.arange(NE_DEV)[None, None, :]
    chosen = jnp.where(column < NE_IN, own_only, anywhere)
    return chosen.reshape(ELNODE, OWNER_TOTAL * NE_DEV).astype(jnp.int32)


def draw_contact_owner(key, part):
    key_star, key_pick, key_order = jax.random.split(key, 3)
    favored = jax.random.randint(key_star, (), 0, OWNER_TOTAL)
    total_slots = OWNER_TOTAL * CAP
    pick_keys = jax.random.split(key_pick, OWNER_TOTAL)
    order_keys = jax.random.split(key_order, OWNER_TOTAL)

    def one_device(pick_key, order_key):
        scores = jax.random.permutation(pick_key, total_slots)
        slot_owner = jnp.arange(total_slots) // CAP
        scores = scores + jnp.where(slot_owner == favored, total_slots, 0)
        top_values, chosen = lax.top_k(scores, CN_DEV)
        chosen = jax.random.permutation(order_key, chosen)
        return (chosen // CAP).astype(jnp.int32)
    return jax.vmap(one_device)(pick_keys, order_keys).reshape(OWNER_TOTAL * CN_DEV).astype(jnp.int32)


def with_ends(values, key, low, top_value):
    index_at = [jax.random.randint(jax.random.fold_in(key, axis), (), 0, length) for axis, length in enumerate(values.shape)]
    widest = values.shape.index(max(values.shape))
    neighbour = index_at[:widest] + [(index_at[widest] + 1) % values.shape[widest]] + index_at[widest + 1:]
    return values.at[tuple(index_at)].set(low).at[tuple(neighbour)].set(top_value)


def levels(own_key, extent, cuts, low, high):
    factor_of, own = 1.0, jax.random.fold_in(own_key, 6)
    for dim, blocks in cuts:
        steps = jnp.exp(jax.random.uniform(jax.random.fold_in(own, dim), (blocks,), jnp.float32, low / len(cuts), high / len(cuts)))
        factor_of = factor_of * jnp.repeat(steps, extent[dim] // blocks).reshape([-1 if axis == dim else 1 for axis in range(len(extent))])
    return factor_of


def normal_values(own_key, shape, deviation, most, shards=(), kind=jnp.bfloat16):
    gain = levels(own_key, shape, shards, -0.22, 0.18) if shards else 1.0
    values = jax.random.normal(own_key, shape, jnp.float32) * deviation * gain
    return jnp.minimum(jnp.maximum(values, -most), most).astype(kind)


def setup_inputs(seed: int = 0) -> dict:
    arg_keys = jax.random.split(jax.random.key(seed), 16)
    displacement = normal_values(arg_keys[0], (3, NODES), 1.0, 6.0, ((1, 32),), jnp.float32)
    disp_prev = normal_values(arg_keys[1], (3, NODES), 1.0, 6.0, ((1, 32),), jnp.float32)
    nodal_load = normal_values(arg_keys[2], (3, NODES), 1.0, 6.0, ((1, 32),), jnp.float32)
    nodal_mass = jnp.clip(jnp.exp(math.log(4.0) - 1.3862944 * jax.random.uniform(arg_keys[3], (NODES,), jnp.float32) ** levels(arg_keys[3], (NODES,), ((0, 32),), -0.2, 0.2)), 1.0, 4.0)
    modulus = jnp.clip(jnp.exp(math.log(10.0) - 2.3025851 * jax.random.uniform(arg_keys[4], (ELEMS,), jnp.float32) ** levels(arg_keys[4], (ELEMS,), ((0, 32),), -0.2, 0.2)), 1.0, 10.0)
    stiffness = draw_stiffness(jax.random.fold_in(arg_keys[15], 71), 0)
    connectivity = draw_connectivity(jax.random.fold_in(arg_keys[15], 71), 0)
    ghost_send = with_ends(jax.random.randint(arg_keys[7], (2, GHOSTS), 0, NODE_DEV), jax.random.fold_in(arg_keys[7], 1), 0, NODE_DEV - 1).astype(jnp.int32)
    contact_node = with_ends(jax.random.randint(arg_keys[8], (CONTACT,), 0, NODE_DEV), jax.random.fold_in(arg_keys[8], 1), 0, NODE_DEV - 1).astype(jnp.int32)
    contact_owner = draw_contact_owner(jax.random.fold_in(arg_keys[15], 71), 0)
    pair_ids = with_ends(jax.random.randint(arg_keys[10], (2, PAIRS), 0, 2 * CN_DEV), jax.random.fold_in(arg_keys[10], 1), 0, (2 * CN_DEV) - 1).astype(jnp.int32)
    gap_start = normal_values(arg_keys[11], (3, PAIRS), 0.5, 3.0, ((1, 32),), jnp.float32)
    penalty = jnp.clip(jnp.exp(math.log(2.0) - 1.3862944 * jax.random.uniform(arg_keys[12], (PAIRS,), jnp.float32) ** levels(arg_keys[12], (PAIRS,), ((0, 32),), -0.2, 0.2)), 0.5, 2.0)
    friction = jnp.clip(0.2 + 0.400000021 * jax.random.uniform(arg_keys[13], (PAIRS,), jnp.float32) ** levels(arg_keys[13], (PAIRS,), ((0, 32),), -0.2, 0.2), 0.2, 0.6)
    slip_state = with_ends((jax.random.randint(arg_keys[14], (STEPS, PAIRS), 0, 3) < 1).astype(jnp.int32), jax.random.fold_in(arg_keys[14], 1), 0, 1)
    return {"displacement": displacement, "disp_prev": disp_prev, "nodal_load": nodal_load, "nodal_mass": nodal_mass, "modulus": modulus, "stiffness": stiffness, "connectivity": connectivity, "ghost_send": ghost_send, "contact_node": contact_node, "contact_owner": contact_owner, "pair_ids": pair_ids, "gap_start": gap_start, "penalty": penalty, "friction": friction, "slip_state": slip_state}


time_step_sq = 0.05

def to_blocks(values, block_width):
    return values.reshape(values.shape[0], OWNER_TOTAL, block_width).transpose(1, 0, 2)

def from_blocks(values):
    return values.transpose(1, 0, 2).reshape(values.shape[1], -1)

def slot_rank(owners):
    onehot = (owners[:, None] == jnp.arange(OWNER_TOTAL, dtype=jnp.int32)[None, :]).astype(jnp.int32)
    earlier = jnp.cumsum(onehot, axis=0) - onehot
    return lax.optimization_barrier(jnp.sum(earlier * onehot, axis=1)).astype(jnp.int32)

def element_forces(extended, node_links, moduli, stiffness):
    gathered = extended[:, node_links].reshape(ELDOF, node_links.shape[1])
    product = jnp.dot(stiffness, gathered, precision=lax.Precision.HIGHEST) * moduli[None, :]
    return jnp.zeros_like(extended).at[:, node_links].add(product.reshape(3, ELNODE, node_links.shape[1]))

def contact_pair_forces(received_values, pair_ids, gap_start, penalty, friction, slipping):
    near_side = received_values[:, pair_ids[0]]
    far_side = received_values[:, pair_ids[1]]
    gap_vec = gap_start + far_side - near_side
    normal = penalty * jnp.maximum(-gap_vec[2], 0.0)
    tangent_gap = gap_vec[0:2]
    sticking = -0.5 * penalty[None, :] * tangent_gap
    length = jnp.sqrt(lax.optimization_barrier(jnp.sum(tangent_gap * tangent_gap, axis=0)) + 0.01)
    sliding = -friction[None, :] * normal[None, :] * tangent_gap / length[None, :]
    tangent = jnp.where(slipping[None, :] == 1, sliding, sticking)
    pair_force = jnp.concatenate([tangent, normal[None, :]], axis=0)
    result = jnp.zeros_like(received_values).at[:, pair_ids[1]].add(pair_force)
    return result.at[:, pair_ids[0]].add(-pair_force)

def lend_nodes(field_now, lend_ids):
    return field_now[:, lend_ids]

def add_ghosts(own_part, lend_ids, from_lower, from_upper):
    return own_part.at[:, lend_ids[0]].add(from_lower).at[:, lend_ids[1]].add(from_upper)

def fill_outbox(field_now, nodes, places):
    return jnp.zeros((3, OWNER_TOTAL * CAP), jnp.float32).at[:, places].set(field_now[:, nodes])

def take_back(returned, nodes, places):
    return jnp.zeros((3, NODE_DEV), jnp.float32).at[:, nodes].add(returned[:, places])

def one_device_forces(device_item, stiffness):
    return element_forces(device_item[0], device_item[1], device_item[2], stiffness)

def swap_owner(values):
    return values.reshape(OWNER_TOTAL, 3, OWNER_TOTAL, CAP).transpose(2, 1, 0, 3).reshape(OWNER_TOTAL, 3, OWNER_TOTAL * CAP)

def reference(displacement, disp_prev, nodal_load, nodal_mass, modulus, stiffness, connectivity, ghost_send, contact_node, contact_owner, pair_ids, gap_start, penalty, friction, slip_state):
    current = to_blocks(displacement, NODE_DEV)
    previous = to_blocks(disp_prev, NODE_DEV)
    loads = to_blocks(nodal_load, NODE_DEV)
    masses = nodal_mass.reshape(OWNER_TOTAL, 1, NODE_DEV)
    node_links = connectivity.reshape(ELNODE, OWNER_TOTAL, NE_DEV).transpose(1, 0, 2)
    moduli = modulus.reshape(OWNER_TOTAL, NE_DEV)
    lend_lists = ghost_send.reshape(2, OWNER_TOTAL, HB).transpose(1, 0, 2)
    contact_nodes = contact_node.reshape(OWNER_TOTAL, CN_DEV)
    contact_owners = contact_owner.reshape(OWNER_TOTAL, CN_DEV)
    places = contact_owners * CAP + jax.vmap(slot_rank)(contact_owners)
    contact_pair_lists = pair_ids.reshape(2, OWNER_TOTAL, PAIRS_PER_OWNER).transpose(1, 0, 2)
    gap_block_parts = to_blocks(gap_start, PAIRS_PER_OWNER)
    penalty_stiffnesses = penalty.reshape(OWNER_TOTAL, PAIRS_PER_OWNER)
    friction_coefficients = friction.reshape(OWNER_TOTAL, PAIRS_PER_OWNER)
    slip_flags = slip_state.reshape(STEPS, OWNER_TOTAL, PAIRS_PER_OWNER)
    blank_rim = jnp.zeros((1, 3, HB), jnp.float32)
    acceleration = current
    for tally_count in range(STEPS):
        outgoing = jax.vmap(lend_nodes)(current, lend_lists)
        lower_ghosts = jnp.concatenate([blank_rim, outgoing[:-1, :, 1]], axis=0)
        upper_ghosts = jnp.concatenate([outgoing[1:, :, 0], blank_rim], axis=0)
        extended = jnp.concatenate([current, lower_ghosts, upper_ghosts], axis=2)
        forces = lax.map(partial_forces(stiffness), (extended, node_links, moduli))
        from_upper = jnp.concatenate([forces[1:, :, NODE_DEV:NODE_DEV + HB], blank_rim], axis=0)
        from_lower = jnp.concatenate([blank_rim, forces[:-1, :, NODE_DEV + HB:]], axis=0)
        internal = jax.vmap(add_ghosts)(forces[:, :, :NODE_DEV], lend_lists, from_lower, from_upper)
        outboxes = jax.vmap(fill_outbox)(current, contact_nodes, places)
        received_values = swap_owner(outboxes)
        reply_messages = jax.vmap(contact_pair_forces)(received_values, contact_pair_lists, gap_block_parts, penalty_stiffnesses, friction_coefficients, slip_flags[tally_count])
        returned = swap_owner(reply_messages)
        contact = jax.vmap(take_back)(returned, contact_nodes, places)
        acceleration = (loads - internal + contact) / masses
        later = 2.0 * current - previous + time_step_sq * acceleration
        previous = current
        current = later
    return (from_blocks(current), from_blocks(acceleration))

def partial_forces(stiffness):

    def apply_one(device_item):
        return one_device_forces(device_item, stiffness)
    return apply_one
```

```python
import functools

import jax
import jax.numpy as jnp
from jax import lax
from jax.experimental import pallas as pl
from jax.experimental.pallas import tpu as pltpu
from jax.sharding import PartitionSpec as P

STEPS = 3
LANES = 128
SUBLANES = 8
PLANES = 4
MESH = pl.DeviceIdType.MESH

time_step_sq = 0.05


def matches(index_row, rows):
    return lax.broadcasted_iota(jnp.int32, (rows, index_row.shape[1]), 0) == index_row


def split(value):
    high = value.astype(jnp.bfloat16).astype(jnp.float32)
    return high, value - high


def contract(left, right):
    return lax.dot_general(
        left, right, (((1,), (1,)), ((), ())), preferred_element_type=jnp.float32
    )


def spread(parts, row_index, rows):
    mask = matches(row_index, rows)
    return jnp.concatenate([jnp.where(mask, part, 0.0) for part in parts], axis=0).astype(
        jnp.bfloat16
    )


def pick(got, lines, row_of, lane_of, r):
    mask = row_of == r
    for c in range(3):
        line = jnp.broadcast_to(lines[c], (SUBLANES, LANES))
        value = jnp.take_along_axis(line, lane_of, axis=1, mode="promise_in_bounds")
        got[c] = jnp.where(mask, value, got[c])


def blank():
    return [jnp.zeros((SUBLANES, LANES), jnp.float32)] * 3


def places_of(index):
    return lax.shift_right_arithmetic(index, 7), index & (LANES - 1)


def kernel(
    dims,
    disp_hbm,
    prev_hbm,
    load_hbm,
    mass_hbm,
    mod_hbm,
    stiff_hbm,
    conn_hbm,
    ghost_hbm,
    node_hbm,
    owner_hbm,
    pair_hbm,
    gap_hbm,
    pen_hbm,
    fric_hbm,
    slip_hbm,
    out_u,
    out_a,
    disp,
    prev,
    load,
    mass,
    mod,
    stiff,
    conn,
    ghost,
    node,
    owner,
    pair,
    gap0,
    pen,
    fric,
    slip,
    row_of_entry,
    lane_hot,
    stiff_parts,
    slot_idx,
    pair_idx,
    lend_idx,
    ue,
    fe,
    acc_e,
    cur,
    old,
    loads,
    gaps,
    slips,
    box_out,
    box_in,
    halo_out,
    halo_in,
    in_sem,
    box_send,
    box_recv,
    halo_send,
    halo_recv,
):
    n_py, n, cap, elnode, lent, width, inner = dims
    px, py = lax.axis_index("px"), lax.axis_index("py")
    me = px * n_py + py

    def place(device):
        return {"px": lax.div(device, n_py), "py": lax.rem(device, n_py)}

    fills = [
        pltpu.make_async_copy(source, target, in_sem.at[i])
        for i, (source, target) in enumerate(
            [
                (owner_hbm, owner),
                (node_hbm, node),
                (disp_hbm, disp),
                (ghost_hbm, ghost),
                (conn_hbm, conn),
                (pair_hbm, pair),
                (stiff_hbm, stiff),
                (mod_hbm, mod),
                (gap_hbm, gap0),
                (slip_hbm, slip),
                (pen_hbm, pen),
                (fric_hbm, fric),
                (prev_hbm, prev),
                (load_hbm, load),
                (mass_hbm, mass),
            ]
        )
    ]
    for fill in fills:
        fill.start()

    barrier = pltpu.get_barrier_semaphore()

    @pl.loop(1, n)
    def _(d):
        pl.semaphore_signal(
            barrier, inc=1, device_id=place(lax.rem(me + d, n)), device_id_type=MESH
        )

    per_plane = n // PLANES
    rows_y = n_py // PLANES
    z, y = lax.div(py, rows_y), lax.rem(py, rows_y)
    half = lax.div(z, 2)
    plane_at = [3 * (1 - half), 2 - half, 1 + 4 * half - z, z]
    my_q = px * rows_y + y
    my_p = (PLANES - 1) * per_plane + my_q

    def device_at(j, q):
        return lax.div(q, rows_y) * n_py + plane_at[j] * rows_y + lax.rem(q, rows_y)

    own_rows = cur.shape[0] // 3
    slot_rows = slot_idx.shape[0]
    plane_rows = slot_rows // PLANES
    per_row = LANES // cap
    wide = ue.shape[0] // 3
    lent_rows = lent // LANES
    ghost_rows = 2 * lent_rows
    chunks = width // LANES
    pair_rows = pair_idx.shape[0] // 2
    pair_groups = pair_rows // chunks
    slot_groups = slot_rows // chunks
    lend = elnode
    near, far = lend + 1, lend + 1 + pair_groups
    first_slot = far + pair_groups

    def set_row(k, row):
        row_of_entry[pl.ds(k, 1), :] = lax.shift_right_arithmetic(row, 7)
        lane_hot[k] = jnp.where(matches(row & (LANES - 1), LANES), 1.0, 0.0).astype(jnp.bfloat16)

    def flat_row(table, first):
        return jnp.concatenate([table[first + i : first + i + 1, :] for i in range(chunks)], axis=1)

    for fill in fills[:2]:
        fill.wait()

    from_lane = lax.broadcasted_iota(jnp.int32, (LANES, 2 * LANES), 0)
    to_lane = lax.broadcasted_iota(jnp.int32, (LANES, 2 * LANES), 1)
    before = jnp.where(from_lane < to_lane, 1.0, 0.0).astype(jnp.bfloat16)
    target = owner[...]
    target_py = lax.rem(target, n_py)
    target_z = lax.div(target_py, rows_y)
    target_j = jnp.where(
        target_z == plane_at[0],
        0,
        jnp.where(target_z == plane_at[1], 1, jnp.where(target_z == plane_at[2], 2, 3)),
    )
    spot = target_j * per_plane + lax.div(target, n_py) * rows_y + lax.rem(target_py, rows_y)
    pieces = owner.shape[0]
    hot = [jnp.where(matches(spot[i : i + 1, :], n), 1.0, 0.0) for i in range(pieces)]
    counts = jnp.dot(
        jnp.concatenate(hot, axis=0).astype(jnp.bfloat16),
        before,
        preferred_element_type=jnp.float32,
    )
    carry = jnp.zeros((n, LANES), jnp.float32)
    ranks = []
    for i in range(pieces):
        earlier = counts[i * n : (i + 1) * n, :LANES]
        ranks.append(jnp.sum(hot[i] * (earlier + carry), axis=0, keepdims=True))
        carry = carry + counts[i * n : (i + 1) * n, LANES:]
    found = jnp.zeros((2 * slot_rows, LANES), jnp.float32)
    for first in range(0, pieces, chunks):
        lefts, rights = [], []
        for i in range(first, first + chunks):
            number = node[i : i + 1, :] + 1
            slot = spot[i : i + 1, :] * cap + ranks[i].astype(jnp.int32)
            parts = [
                lax.shift_right_arithmetic(number, 6).astype(jnp.float32),
                (number & 63).astype(jnp.float32),
            ]
            lefts.append(spread(parts, lax.shift_right_arithmetic(slot, 7), slot_rows))
            rights.append(
                jnp.where(matches(slot & (LANES - 1), LANES), 1.0, 0.0).astype(jnp.bfloat16)
            )
        found = found + contract(
            jnp.concatenate(lefts, axis=1), jnp.concatenate(rights, axis=1)
        )
    slot_idx[...] = (found[:slot_rows] * 64.0 + found[slot_rows:]).astype(jnp.int32) - 1

    for fill in fills[2:4]:
        fill.wait()

    def to_rows(table, source, rows):
        for c in range(3):
            for r in range(rows):
                table[c * rows + r : c * rows + r + 1, :] = source[
                    c : c + 1, r * LANES : (r + 1) * LANES
                ]

    to_rows(cur, disp, own_rows)
    lend_idx[...] = jnp.full_like(lend_idx, -1)
    for side in range(2):
        for r in range(lent_rows):
            at = side * lent_rows + r
            lend_idx[at : at + 1, :] = ghost[side : side + 1, r * LANES : (r + 1) * LANES]

    def box_copy(i, there, spot_out):
        return pltpu.make_async_remote_copy(
            src_ref=box_out.at[i, spot_out],
            dst_ref=box_in.at[i, me],
            send_sem=box_send.at[i],
            recv_sem=box_recv.at[i, z],
            device_id=place(there),
            device_id_type=MESH,
        )

    def box_bytes(i, count, plane):
        every = pl.ds(0, count)
        return pltpu.make_async_remote_copy(
            src_ref=box_out.at[i, every],
            dst_ref=box_in.at[i, every],
            send_sem=box_send.at[i],
            recv_sem=box_recv.at[i, plane],
            device_id=place(lax.rem(me + 1, n)),
            device_id_type=MESH,
        )

    def box_start(i, j, by_device):
        for d in range(1 if j == PLANES - 1 else 0, per_plane):
            q = lax.rem(my_q + d, per_plane)
            there = device_at(j, q)
            box_copy(i, there, there if by_device else j * per_plane + q).start()

    def box_wait(i, j):
        own = 1 if j == PLANES - 1 else 0
        box_bytes(i, per_plane - own, plane_at[j]).wait_recv()

    def halo_copies(i):
        copies = []
        for side, step in ((0, n - 1), (1, 1)):
            copies.append(
                pltpu.make_async_remote_copy(
                    src_ref=halo_out.at[i, side],
                    dst_ref=halo_in.at[i, 1 - side],
                    send_sem=halo_send.at[i, side],
                    recv_sem=halo_recv.at[i, 1 - side],
                    device_id=place(lax.rem(me + step, n)),
                    device_id_type=MESH,
                )
            )
        return copies

    def halo_start(i):
        for copy in halo_copies(i):
            copy.start()

    def halo_wait(i):
        for copy in halo_copies(i):
            copy.wait_recv()

    def halo_side(i, side, c):
        inside = me > 0 if side == 0 else me < n - 1
        return jnp.where(inside, halo_in[i, side, c : c + 1, :], 0.0)

    def box_row(i, devices):
        boxes = [box_in[i, device] for device in devices]
        return boxes[0] if per_row == 1 else jnp.concatenate(boxes, axis=1)

    def table_lines(table, rows, r):
        return [table[c * rows + r : c * rows + r + 1, :] for c in range(3)]

    for step in range(STEPS):
        going, back = 2 * step, 2 * step + 1

        row_of, lane_of = places_of(lend_idx[...])
        got = blank()
        for r in range(own_rows):
            pick(got, table_lines(cur, own_rows, r), row_of, lane_of, r)
        for c in range(3):
            for side in range(2):
                for r in range(lent_rows):
                    at = side * lent_rows + r
                    halo_out[going, side, c : c + 1, r * LANES : (r + 1) * LANES] = got[c][
                        at : at + 1
                    ]
        if step == 0:
            pl.semaphore_wait(barrier, n - 1)
        halo_start(going)

        for j in range(PLANES):
            row_of, lane_of = places_of(slot_idx[j * plane_rows : (j + 1) * plane_rows, :])
            got = blank()
            for r in range(own_rows):
                pick(got, table_lines(cur, own_rows, r), row_of, lane_of, r)
            for q in range(per_plane):
                r, l = divmod(q * cap, LANES)
                for c in range(3):
                    box_out[going, j * per_plane + q, c : c + 1, :] = got[c][
                        r : r + 1, l : l + cap
                    ]
            box_start(going, j, False)
        box_in[going, me] = box_out[going, my_p]

        if step == 0:
            for fill in fills[4:]:
                fill.wait()

            @pl.loop(0, elnode)
            def _(k):
                set_row(k, conn[pl.ds(k, 1), :])

            for i in range(2):
                for r in range(pair_rows):
                    pair_idx[i * pair_rows + r : i * pair_rows + r + 1, :] = pair[
                        i : i + 1, r * LANES : (r + 1) * LANES
                    ]
            for i, first in ((0, near), (1, far)):
                for h in range(pair_groups):
                    set_row(first + h, pair[i : i + 1, h * width : (h + 1) * width])
            set_row(lend, flat_row(lend_idx, 0))
            to_rows(gaps, gap0, pair_rows)
            to_rows(slips, slip, pair_rows)
            to_rows(old, prev, own_rows)
            to_rows(loads, load, own_rows)
            ue[...] = jnp.zeros_like(ue)
            stiff_parts[...] = jnp.zeros_like(stiff_parts)
            for c in range(3):
                for d in range(3):
                    block = stiff[c * elnode : (c + 1) * elnode, d * elnode : (d + 1) * elnode]
                    high, low = split(block)
                    for at, part in ((0, high), (1, high), (2, low)):
                        start = (3 * at + d) * wide
                        stiff_parts[c * wide : c * wide + elnode, start : start + elnode] = part

        def forces(cols):
            high, low = split(ue[:, cols])
            right = jnp.concatenate([high, low, high], axis=0).astype(jnp.bfloat16)
            left = stiff_parts[...].astype(jnp.bfloat16)
            product = jnp.dot(left, right, preferred_element_type=jnp.float32) * mod[:, cols]
            high, low = split(product)
            fe[0, :, cols] = high
            fe[1, :, cols] = low

        tops = [min(k, elnode - SUBLANES) for k in range(0, elnode, SUBLANES)]

        @pl.loop(0, chunks)
        def _(i):
            lanes = pl.ds(pl.multiple_of(i * LANES, LANES), LANES)
            for top in tops:
                row_of, lane_of = places_of(conn[top : top + SUBLANES, lanes])
                got = blank()
                for r in range(own_rows):
                    pick(got, table_lines(cur, own_rows, r), row_of, lane_of, r)
                for c in range(3):
                    ue[c * wide + top : c * wide + top + SUBLANES, lanes] = got[c]

        forces(slice(0, inner))

        pair_at = [places_of(pair_idx[i * pair_rows : (i + 1) * pair_rows, :]) for i in range(2)]
        ends = [blank(), blank()]

        def pair_pick(j):
            for q in range(0, per_plane, per_row):
                devices = [device_at(j, q + t) for t in range(per_row)]
                box = box_row(going, devices)
                lines = [box[c : c + 1, :] for c in range(3)]
                row = lax.div(devices[0], per_row)
                for i in range(2):
                    pick(ends[i], lines, *pair_at[i], row)

        for j in range(PLANES - 1, 0, -1):
            box_wait(going, j)
            pair_pick(j)

        halo_wait(going)
        ghosts = [[halo_side(going, side, c) for c in range(3)] for side in range(2)]
        for top in tops:
            row_of, lane_of = places_of(conn[top : top + SUBLANES, inner:])
            for b in range((width - inner) // LANES):
                lanes = slice(b * LANES, (b + 1) * LANES)
                spots = slice(inner + b * LANES, inner + (b + 1) * LANES)
                got = [ue[c * wide + top : c * wide + top + SUBLANES, spots] for c in range(3)]
                for side in range(2):
                    for r in range(lent_rows):
                        lines = [
                            ghosts[side][c][:, r * LANES : (r + 1) * LANES] for c in range(3)
                        ]
                        at = own_rows + side * lent_rows + r
                        pick(got, lines, row_of[:, lanes], lane_of[:, lanes], at)
                for c in range(3):
                    ue[c * wide + top : c * wide + top + SUBLANES, spots] = got[c]
        forces(slice(inner, width))

        edge = jnp.zeros((6 * ghost_rows, LANES), jnp.float32)
        for first in range(0, elnode, chunks):
            lefts, rights = [], []
            for k in range(first, min(first + chunks, elnode)):
                row = row_of_entry[k : k + 1, inner:] - own_rows
                parts = [
                    fe[s, c * wide + k : c * wide + k + 1, inner:] for s in range(2) for c in range(3)
                ]
                lefts.append(spread(parts, row, ghost_rows))
                rights.append(lane_hot[k, :, inner:])
            edge = edge + contract(
                jnp.concatenate(lefts, axis=1), jnp.concatenate(rights, axis=1)
            )
        edge = edge[: 3 * ghost_rows] + edge[3 * ghost_rows :]
        for c in range(3):
            for side in range(2):
                for r in range(lent_rows):
                    at = c * ghost_rows + side * lent_rows + r
                    halo_out[back, side, c : c + 1, r * LANES : (r + 1) * LANES] = edge[at : at + 1]
        halo_start(back)

        box_wait(going, 0)
        pair_pick(0)
        gap = [
            gaps[c * pair_rows : (c + 1) * pair_rows, :] + ends[1][c] - ends[0][c] for c in range(3)
        ]
        normal = pen[...] * jnp.maximum(-gap[2], 0.0)
        length = jnp.sqrt(gap[0] * gap[0] + gap[1] * gap[1] + 0.01)
        slipping = slips[step * pair_rows : (step + 1) * pair_rows, :] == 1
        factor = jnp.where(slipping, -fric[...] * normal / length, -0.5 * pen[...])
        force = [factor * gap[0], factor * gap[1], normal]
        halves = [split(value) for value in force]
        total = jnp.zeros((6 * slot_rows, LANES), jnp.float32)
        for sign, first in ((1.0, far), (-1.0, near)):
            for h in range(pair_groups):
                parts = [
                    flat_row(sign * halves[c][s], h * chunks) for s in range(2) for c in range(3)
                ]
                k = first + h
                total = total + contract(
                    spread(parts, row_of_entry[k : k + 1, :], slot_rows), lane_hot[k]
                )
        total = total[: 3 * slot_rows] + total[3 * slot_rows :]
        for g in range(n):
            r, l = divmod(g * cap, LANES)
            for c in range(3):
                at = c * slot_rows + r
                box_out[back, g, c : c + 1, :] = total[at : at + 1, l : l + cap]
        for j in range(PLANES):
            box_start(back, j, True)
        box_in[back, me] = box_out[back, me]

        if step == 0:
            for m in range(slot_groups):
                set_row(first_slot + m, flat_row(slot_idx, m * chunks))

        acc_e[...] = jnp.zeros_like(acc_e)
        some = next(f for f in (9, 3, 1) if elnode % f == 0)

        @pl.loop(0, elnode // some)
        def _(group):
            total = acc_e[...]
            for i in range(some):
                k = group * some + i
                parts = [
                    fe[s, pl.ds(c * wide + k, 1), :] for s in range(2) for c in range(3)
                ]
                total = total + contract(
                    spread(parts, row_of_entry[pl.ds(k, 1), :], own_rows), lane_hot[k]
                )
            acc_e[...] = total

        contact = jnp.zeros((6 * own_rows, LANES), jnp.float32)
        groups = plane_rows // chunks
        for j in range(PLANES - 1, -1, -1):
            if j == 0:
                halo_wait(back)
                values = [
                    jnp.concatenate([halo_side(back, 0, c), halo_side(back, 1, c)], axis=1)
                    for c in range(3)
                ]
                halves = [split(-value) for value in values]
                parts = [halves[c][s] for s in range(2) for c in range(3)]
                contact = contact + contract(
                    spread(parts, row_of_entry[lend : lend + 1, :], own_rows), lane_hot[lend]
                )
            box_wait(back, j)
            for m in range(groups):
                boxes = []
                for i in range(chunks):
                    q = (m * chunks + i) * per_row
                    boxes.append(
                        box_row(back, [device_at(j, q + t) for t in range(per_row)])
                    )
                halves = split(jnp.concatenate(boxes, axis=1))
                parts = [halves[s][c : c + 1, :] for s in range(2) for c in range(3)]
                k = first_slot + j * groups + m
                contact = contact + contract(
                    spread(parts, row_of_entry[k : k + 1, :], own_rows), lane_hot[k]
                )

        total = contact - acc_e[...]
        total = total[: 3 * own_rows] + total[3 * own_rows :]
        for c in range(3):
            rows = slice(c * own_rows, (c + 1) * own_rows)
            acceleration = (loads[rows, :] + total[rows]) / mass[...]
            now = cur[rows, :]
            later = 2.0 * now - old[rows, :] + time_step_sq * acceleration
            if step == STEPS - 1:
                out_u[rows, :] = later
                out_a[rows, :] = acceleration
            else:
                old[rows, :] = now
                cur[rows, :] = later

    for i in range(2 * STEPS):
        box_bytes(i, n - 1, 0).wait_send()
        for copy in halo_copies(i):
            copy.wait_send()


def on_device(
    n_py,
    displacement,
    disp_prev,
    nodal_load,
    nodal_mass,
    modulus,
    stiffness,
    connectivity,
    ghost_send,
    contact_node,
    contact_owner,
    pair_ids,
    gap_start,
    penalty,
    friction,
    slip_state,
):
    n = lax.axis_size(("px", "py"))
    cap = 2 * contact_node.shape[0] // n
    elnode, width = connectivity.shape
    nodes = displacement.shape[1]
    lent = ghost_send.shape[1]
    own_rows = nodes // LANES
    slot_rows = n * cap // LANES
    wide = -(-elnode // SUBLANES) * SUBLANES
    pair_rows = pair_ids.shape[1] // LANES
    slot_groups = slot_rows * LANES // width
    pair_groups = pair_ids.shape[1] // width
    inner = width * 3 // 4
    entries = elnode + 1 + 2 * pair_groups + slot_groups
    flat = (3 * own_rows, LANES)
    vmem = pl.BlockSpec(memory_space=pltpu.VMEM)
    hbm = pl.BlockSpec(memory_space=pltpu.HBM)
    f32, bf16, i32 = jnp.float32, jnp.bfloat16, jnp.int32
    dma = pltpu.SemaphoreType.DMA
    args = [
        displacement,
        disp_prev,
        nodal_load,
        nodal_mass.reshape(-1, LANES),
        modulus.reshape(1, -1),
        stiffness,
        connectivity,
        ghost_send,
        contact_node.reshape(-1, LANES),
        contact_owner.reshape(-1, LANES),
        pair_ids,
        gap_start,
        penalty.reshape(-1, LANES),
        friction.reshape(-1, LANES),
        slip_state,
    ]
    new_u, acc = pl.pallas_call(
        functools.partial(kernel, (n_py, n, cap, elnode, lent, width, inner)),
        out_shape=[jax.ShapeDtypeStruct(flat, f32)] * 2,
        in_specs=[hbm] * len(args),
        out_specs=[vmem] * 2,
        scratch_shapes=[pltpu.VMEM(a.shape, a.dtype) for a in args]
        + [
            pltpu.VMEM((entries, width), i32),
            pltpu.VMEM((entries, LANES, width), bf16),
            pltpu.VMEM((3 * wide, 9 * wide), f32),
            pltpu.VMEM((slot_rows, LANES), i32),
            pltpu.VMEM((2 * pair_rows, LANES), i32),
            pltpu.VMEM((SUBLANES, LANES), i32),
            pltpu.VMEM((3 * wide, width), f32),
            pltpu.VMEM((2, 3 * wide, width), f32),
            pltpu.VMEM((6 * own_rows, LANES), f32),
            pltpu.VMEM(flat, f32),
            pltpu.VMEM(flat, f32),
            pltpu.VMEM(flat, f32),
            pltpu.VMEM((3 * pair_rows, LANES), f32),
            pltpu.VMEM((3 * pair_rows, LANES), i32),
            pltpu.VMEM((2 * STEPS, n, 3, cap), f32),
            pltpu.VMEM((2 * STEPS, n, 3, cap), f32),
            pltpu.VMEM((2 * STEPS, 2, 3, lent), f32),
            pltpu.VMEM((2 * STEPS, 2, 3, lent), f32),
            dma((len(args),)),
            dma((2 * STEPS,)),
            dma((2 * STEPS, PLANES)),
            dma((2 * STEPS, 2)),
            dma((2 * STEPS, 2)),
        ],
        compiler_params=pltpu.CompilerParams(
            collective_id=0, has_side_effects=True, vmem_limit_bytes=48 * 1024 * 1024
        ),
        name="contact_steps",
    )(*args)
    return new_u.reshape(displacement.shape), acc.reshape(displacement.shape)


def solution(mesh):
    both = ("px", "py")
    row, cols = P(both), P(None, both)
    return jax.shard_map(
        functools.partial(on_device, mesh.shape["py"]),
        mesh=mesh,
        in_specs=(cols, cols, cols, row, row, P(), cols, cols, row, row, cols, cols, row, row, cols),
        out_specs=(cols, cols),
        check_vma=False,
    )
```

```python
import functools

import jax
import jax.numpy as jnp
from jax import lax
from jax.experimental import pallas as pl
from jax.experimental.pallas import tpu as pltpu
from jax.sharding import PartitionSpec as P

STEPS = 3
LANES = 128
SUBLANES = 8
PLANES = 4
MESH = pl.DeviceIdType.MESH

time_step_sq = 0.05


def matches(index_row, rows):
    return lax.broadcasted_iota(jnp.int32, (rows, index_row.shape[1]), 0) == index_row


def split(value):
    high = value.astype(jnp.bfloat16).astype(jnp.float32)
    return high, value - high


def contract(left, right):
    return lax.dot_general(
        left, right, (((1,), (1,)), ((), ())), preferred_element_type=jnp.float32
    )


def spread(parts, row_index, rows):
    mask = matches(row_index, rows)
    return jnp.concatenate([jnp.where(mask, part, 0.0) for part in parts], axis=0).astype(
        jnp.bfloat16
    )


def pick(got, lines, row_of, lane_of, r):
    mask = row_of == r
    for c in range(3):
        line = jnp.broadcast_to(lines[c], (SUBLANES, LANES))
        value = jnp.take_along_axis(line, lane_of, axis=1, mode="promise_in_bounds")
        got[c] = jnp.where(mask, value, got[c])


def blank():
    return [jnp.zeros((SUBLANES, LANES), jnp.float32)] * 3


def places_of(index):
    return lax.shift_right_arithmetic(index, 7), index & (LANES - 1)


def kernel(
    dims,
    disp_hbm,
    prev_hbm,
    load_hbm,
    mass_hbm,
    mod_hbm,
    stiff_hbm,
    conn_hbm,
    ghost_hbm,
    node_hbm,
    owner_hbm,
    pair_hbm,
    gap_hbm,
    pen_hbm,
    fric_hbm,
    slip_hbm,
    out_u,
    out_a,
    disp,
    prev,
    load,
    mass,
    mod,
    stiff,
    conn,
    ghost,
    node,
    owner,
    pair,
    gap0,
    pen,
    fric,
    slip,
    row_of_entry,
    lane_hot,
    stiff_parts,
    slot_idx,
    pair_idx,
    lend_idx,
    ue,
    fe,
    acc_e,
    cur,
    old,
    loads,
    gaps,
    slips,
    box_out,
    box_in,
    halo_out,
    halo_in,
    in_sem,
    box_send,
    box_recv,
    halo_send,
    halo_recv,
):
    n_py, n, cap, elnode, lent, width, inner = dims
    px, py = lax.axis_index("px"), lax.axis_index("py")
    me = px * n_py + py

    def place(device):
        return {"px": lax.div(device, n_py), "py": lax.rem(device, n_py)}

    fills = [
        pltpu.make_async_copy(source, target, in_sem.at[i])
        for i, (source, target) in enumerate(
            [
                (owner_hbm, owner),
                (node_hbm, node),
                (disp_hbm, disp),
                (ghost_hbm, ghost),
                (conn_hbm, conn),
                (pair_hbm, pair),
                (stiff_hbm, stiff),
                (mod_hbm, mod),
                (gap_hbm, gap0),
                (slip_hbm, slip),
                (pen_hbm, pen),
                (fric_hbm, fric),
                (prev_hbm, prev),
                (load_hbm, load),
                (mass_hbm, mass),
            ]
        )
    ]
    for fill in fills:
        fill.start()

    barrier = pltpu.get_barrier_semaphore()

    @pl.loop(1, n)
    def _(d):
        pl.semaphore_signal(
            barrier, inc=1, device_id=place(lax.rem(me + d, n)), device_id_type=MESH
        )

    per_plane = n // PLANES
    rows_y = n_py // PLANES
    rows_x = n // n_py // 2
    z, y = lax.div(py, rows_y), lax.rem(py, rows_y)
    x, core = lax.div(px, 2), lax.rem(px, 2)
    half = lax.div(z, 2)
    plane_at = [3 * (1 - half), 2 - half, 1 + 4 * half - z, z]
    turns = sorted(
        [(a, e, b) for a in range(rows_x) for e in range(2) for b in range(rows_y)],
        key=lambda t: min(t[0], rows_x - t[0]) + min(t[2], rows_y - t[2]) + 1 - t[1],
        reverse=True,
    )
    my_q = turns.index((0, 0, 0))
    my_p = (PLANES - 1) * per_plane + my_q
    columns = [
        (lax.rem(x + a, rows_x) * 2 + lax.rem(core + e, 2)) * n_py + lax.rem(y + b, rows_y)
        for a, e, b in turns
    ]

    def device_at(j, q):
        return columns[q] + plane_at[j] * rows_y

    own_rows = cur.shape[0] // 3
    slot_rows = slot_idx.shape[0]
    plane_rows = slot_rows // PLANES
    per_row = LANES // cap
    wide = ue.shape[0] // 3
    lent_rows = lent // LANES
    ghost_rows = 2 * lent_rows
    chunks = width // LANES
    pair_rows = pair_idx.shape[0] // 2
    pair_groups = pair_rows // chunks
    slot_groups = slot_rows // chunks
    lend = elnode
    near, far = lend + 1, lend + 1 + pair_groups
    first_slot = far + pair_groups

    def set_row(k, row):
        row_of_entry[pl.ds(k, 1), :] = lax.shift_right_arithmetic(row, 7)
        lane_hot[k] = jnp.where(matches(row & (LANES - 1), LANES), 1.0, 0.0).astype(jnp.bfloat16)

    def flat_row(table, first):
        return jnp.concatenate([table[first + i : first + i + 1, :] for i in range(chunks)], axis=1)

    for fill in fills[:2]:
        fill.wait()

    from_lane = lax.broadcasted_iota(jnp.int32, (LANES, 2 * LANES), 0)
    to_lane = lax.broadcasted_iota(jnp.int32, (LANES, 2 * LANES), 1)
    before = jnp.where(from_lane < to_lane, 1.0, 0.0).astype(jnp.bfloat16)
    target = owner[...]
    target_py = lax.rem(target, n_py)
    target_z = lax.div(target_py, rows_y)
    target_j = jnp.where(
        target_z == plane_at[0],
        0,
        jnp.where(target_z == plane_at[1], 1, jnp.where(target_z == plane_at[2], 2, 3)),
    )
    target_px = lax.div(target, n_py)
    a = lax.rem(lax.div(target_px, 2) - x + rows_x, rows_x)
    e = lax.rem(lax.rem(target_px, 2) - core + 2, 2)
    b = lax.rem(lax.rem(target_py, rows_y) - y + rows_y, rows_y)
    turn = (a * 2 + e) * rows_y + b
    spot = target_j * per_plane
    for q, (a, e, b) in enumerate(turns):
        spot = spot + jnp.where(turn == (a * 2 + e) * rows_y + b, q, 0)
    pieces = owner.shape[0]
    hot = [jnp.where(matches(spot[i : i + 1, :], n), 1.0, 0.0) for i in range(pieces)]
    counts = jnp.dot(
        jnp.concatenate(hot, axis=0).astype(jnp.bfloat16),
        before,
        preferred_element_type=jnp.float32,
    )
    carry = jnp.zeros((n, LANES), jnp.float32)
    ranks = []
    for i in range(pieces):
        earlier = counts[i * n : (i + 1) * n, :LANES]
        ranks.append(jnp.sum(hot[i] * (earlier + carry), axis=0, keepdims=True))
        carry = carry + counts[i * n : (i + 1) * n, LANES:]
    found = jnp.zeros((2 * slot_rows, LANES), jnp.float32)
    for first in range(0, pieces, chunks):
        lefts, rights = [], []
        for i in range(first, first + chunks):
            number = node[i : i + 1, :] + 1
            slot = spot[i : i + 1, :] * cap + ranks[i].astype(jnp.int32)
            parts = [
                lax.shift_right_arithmetic(number, 6).astype(jnp.float32),
                (number & 63).astype(jnp.float32),
            ]
            lefts.append(spread(parts, lax.shift_right_arithmetic(slot, 7), slot_rows))
            rights.append(
                jnp.where(matches(slot & (LANES - 1), LANES), 1.0, 0.0).astype(jnp.bfloat16)
            )
        found = found + contract(
            jnp.concatenate(lefts, axis=1), jnp.concatenate(rights, axis=1)
        )
    slot_idx[...] = (found[:slot_rows] * 64.0 + found[slot_rows:]).astype(jnp.int32) - 1

    for fill in fills[2:4]:
        fill.wait()

    def to_rows(table, source, rows):
        for c in range(3):
            for r in range(rows):
                table[c * rows + r : c * rows + r + 1, :] = source[
                    c : c + 1, r * LANES : (r + 1) * LANES
                ]

    to_rows(cur, disp, own_rows)
    lend_idx[...] = jnp.full_like(lend_idx, -1)
    for side in range(2):
        for r in range(lent_rows):
            at = side * lent_rows + r
            lend_idx[at : at + 1, :] = ghost[side : side + 1, r * LANES : (r + 1) * LANES]

    def box_copy(i, there, spot_out, kind):
        return pltpu.make_async_remote_copy(
            src_ref=box_out.at[i, spot_out],
            dst_ref=box_in.at[i, me],
            send_sem=box_send.at[i],
            recv_sem=box_recv.at[i, z, kind],
            device_id=place(there),
            device_id_type=MESH,
        )

    def box_bytes(i, count, plane, kind):
        every = pl.ds(0, count)
        return pltpu.make_async_remote_copy(
            src_ref=box_out.at[i, every],
            dst_ref=box_in.at[i, every],
            send_sem=box_send.at[i],
            recv_sem=box_recv.at[i, plane, kind],
            device_id=place(lax.rem(me + 1, n)),
            device_id_type=MESH,
        )

    def box_start(i, j, by_device):
        for q in range(per_plane):
            if j < PLANES - 1 or q != my_q:
                there = device_at(j, q)
                spot_out = there if by_device else j * per_plane + q
                box_copy(i, there, spot_out, 0 if q == 0 else 1).start()

    def wait_first(i, j):
        box_bytes(i, 1, plane_at[j], 0).wait_recv()

    def wait_rest(i, j):
        own = 1 if j == PLANES - 1 else 0
        box_bytes(i, per_plane - 1 - own, plane_at[j], 1).wait_recv()

    def halo_copies(i):
        copies = []
        for side, step in ((0, n - 1), (1, 1)):
            copies.append(
                pltpu.make_async_remote_copy(
                    src_ref=halo_out.at[i, side],
                    dst_ref=halo_in.at[i, 1 - side],
                    send_sem=halo_send.at[i, side],
                    recv_sem=halo_recv.at[i, 1 - side],
                    device_id=place(lax.rem(me + step, n)),
                    device_id_type=MESH,
                )
            )
        return copies

    def halo_start(i):
        for copy in halo_copies(i):
            copy.start()

    def halo_wait(i):
        for copy in halo_copies(i):
            copy.wait_recv()

    def halo_side(i, side, c):
        inside = me > 0 if side == 0 else me < n - 1
        return jnp.where(inside, halo_in[i, side, c : c + 1, :], 0.0)

    def box_row(i, devices):
        boxes = [box_in[i, device] for device in devices]
        return boxes[0] if per_row == 1 else jnp.concatenate(boxes, axis=1)

    def table_lines(table, rows, r):
        return [table[c * rows + r : c * rows + r + 1, :] for c in range(3)]

    for step in range(STEPS):
        going, back = 2 * step, 2 * step + 1

        def send_plane(j):
            row_of, lane_of = places_of(slot_idx[j * plane_rows : (j + 1) * plane_rows, :])
            got = blank()
            for r in range(own_rows):
                pick(got, table_lines(cur, own_rows, r), row_of, lane_of, r)
            for q in range(per_plane):
                r, l = divmod(q * cap, LANES)
                for c in range(3):
                    box_out[going, j * per_plane + q, c : c + 1, :] = got[c][
                        r : r + 1, l : l + cap
                    ]
            if step == 0 and j == 0:
                pl.semaphore_wait(barrier, n - 1)
            box_start(going, j, False)

        send_plane(0)
        row_of, lane_of = places_of(lend_idx[...])
        got = blank()
        for r in range(own_rows):
            pick(got, table_lines(cur, own_rows, r), row_of, lane_of, r)
        for c in range(3):
            for side in range(2):
                for r in range(lent_rows):
                    at = side * lent_rows + r
                    halo_out[going, side, c : c + 1, r * LANES : (r + 1) * LANES] = got[c][
                        at : at + 1
                    ]
        halo_start(going)
        for j in range(1, PLANES):
            send_plane(j)
        box_in[going, me] = box_out[going, my_p]

        if step == 0:
            for fill in fills[4:]:
                fill.wait()

            @pl.loop(0, elnode)
            def _(k):
                set_row(k, conn[pl.ds(k, 1), :])

            for i in range(2):
                for r in range(pair_rows):
                    pair_idx[i * pair_rows + r : i * pair_rows + r + 1, :] = pair[
                        i : i + 1, r * LANES : (r + 1) * LANES
                    ]
            for i, first in ((0, near), (1, far)):
                for h in range(pair_groups):
                    set_row(first + h, pair[i : i + 1, h * width : (h + 1) * width])
            set_row(lend, flat_row(lend_idx, 0))
            to_rows(gaps, gap0, pair_rows)
            to_rows(slips, slip, pair_rows)
            to_rows(old, prev, own_rows)
            to_rows(loads, load, own_rows)
            mass[...] = 1.0 / mass[...]
            ue[...] = jnp.zeros_like(ue)
            stiff_parts[...] = jnp.zeros_like(stiff_parts)
            for c in range(3):
                for d in range(3):
                    block = stiff[c * elnode : (c + 1) * elnode, d * elnode : (d + 1) * elnode]
                    high, low = split(block)
                    for at, part in ((0, high), (1, high), (2, low)):
                        start = (3 * at + d) * wide
                        stiff_parts[c * wide : c * wide + elnode, start : start + elnode] = part

        def forces(cols):
            high, low = split(ue[:, cols])
            right = jnp.concatenate([high, low, high], axis=0).astype(jnp.bfloat16)
            left = stiff_parts[...].astype(jnp.bfloat16)
            product = jnp.dot(left, right, preferred_element_type=jnp.float32) * mod[:, cols]
            high, low = split(product)
            fe[0, :, cols] = high
            fe[1, :, cols] = low

        tops = [min(k, elnode - SUBLANES) for k in range(0, elnode, SUBLANES)]

        @pl.loop(0, chunks)
        def _(i):
            lanes = pl.ds(pl.multiple_of(i * LANES, LANES), LANES)
            for top in tops:
                row_of, lane_of = places_of(conn[top : top + SUBLANES, lanes])
                got = blank()
                for r in range(own_rows):
                    pick(got, table_lines(cur, own_rows, r), row_of, lane_of, r)
                for c in range(3):
                    ue[c * wide + top : c * wide + top + SUBLANES, lanes] = got[c]

        forces(slice(0, inner))

        pair_at = [places_of(pair_idx[i * pair_rows : (i + 1) * pair_rows, :]) for i in range(2)]
        ends = [blank(), blank()]

        def pair_pick(lines_of, row):
            for i in range(2):
                pick(ends[i], lines_of, *pair_at[i], row)

        def pair_picks(j, places):
            for q in places:
                there = device_at(j, q)
                pair_pick([box_in[going, there, c : c + 1, :] for c in range(3)], there)

        if per_row == 1:
            for j in range(PLANES - 1, 0, -1):
                wait_first(going, j)
                wait_rest(going, j)
                pair_picks(j, range(per_plane))
            wait_rest(going, 0)
            pair_picks(0, range(1, per_plane))

        halo_wait(going)
        ghosts = [[halo_side(going, side, c) for c in range(3)] for side in range(2)]
        for top in tops:
            row_of, lane_of = places_of(conn[top : top + SUBLANES, inner:])
            for b in range((width - inner) // LANES):
                lanes = slice(b * LANES, (b + 1) * LANES)
                spots = slice(inner + b * LANES, inner + (b + 1) * LANES)
                got = [ue[c * wide + top : c * wide + top + SUBLANES, spots] for c in range(3)]
                for side in range(2):
                    for r in range(lent_rows):
                        lines = [
                            ghosts[side][c][:, r * LANES : (r + 1) * LANES] for c in range(3)
                        ]
                        at = own_rows + side * lent_rows + r
                        pick(got, lines, row_of[:, lanes], lane_of[:, lanes], at)
                for c in range(3):
                    ue[c * wide + top : c * wide + top + SUBLANES, spots] = got[c]
        forces(slice(inner, width))

        if per_row == 1:
            wait_first(going, 0)
            pair_picks(0, range(1))
        else:
            for j in range(PLANES):
                wait_first(going, j)
                wait_rest(going, j)
            for r in range(slot_rows):
                box = box_row(going, [r * per_row + t for t in range(per_row)])
                pair_pick([box[c : c + 1, :] for c in range(3)], r)
        gap = [
            gaps[c * pair_rows : (c + 1) * pair_rows, :] + ends[1][c] - ends[0][c] for c in range(3)
        ]
        normal = pen[...] * jnp.maximum(-gap[2], 0.0)
        length = jnp.sqrt(gap[0] * gap[0] + gap[1] * gap[1] + 0.01)
        slipping = slips[step * pair_rows : (step + 1) * pair_rows, :] == 1
        factor = jnp.where(slipping, -fric[...] * normal / length, -0.5 * pen[...])
        force = [factor * gap[0], factor * gap[1], normal]
        halves = [split(value) for value in force]
        total = jnp.zeros((6 * slot_rows, LANES), jnp.float32)
        for sign, first in ((1.0, far), (-1.0, near)):
            for h in range(pair_groups):
                parts = [
                    flat_row(sign * halves[c][s], h * chunks) for s in range(2) for c in range(3)
                ]
                k = first + h
                total = total + contract(
                    spread(parts, row_of_entry[k : k + 1, :], slot_rows), lane_hot[k]
                )
        total = total[: 3 * slot_rows] + total[3 * slot_rows :]
        for g in range(n):
            r, l = divmod(g * cap, LANES)
            for c in range(3):
                at = c * slot_rows + r
                box_out[back, g, c : c + 1, :] = total[at : at + 1, l : l + cap]
        for j in range(PLANES):
            box_start(back, j, True)
        box_in[back, me] = box_out[back, me]

        edge = jnp.zeros((6 * ghost_rows, LANES), jnp.float32)
        for first in range(0, elnode, chunks):
            lefts, rights = [], []
            for k in range(first, min(first + chunks, elnode)):
                row = row_of_entry[k : k + 1, inner:] - own_rows
                parts = [
                    fe[s, c * wide + k : c * wide + k + 1, inner:] for s in range(2) for c in range(3)
                ]
                lefts.append(spread(parts, row, ghost_rows))
                rights.append(lane_hot[k, :, inner:])
            edge = edge + contract(
                jnp.concatenate(lefts, axis=1), jnp.concatenate(rights, axis=1)
            )
        edge = edge[: 3 * ghost_rows] + edge[3 * ghost_rows :]
        for c in range(3):
            for side in range(2):
                for r in range(lent_rows):
                    at = c * ghost_rows + side * lent_rows + r
                    halo_out[back, side, c : c + 1, r * LANES : (r + 1) * LANES] = edge[at : at + 1]
        halo_start(back)

        if step == 0:
            for m in range(slot_groups):
                set_row(first_slot + m, flat_row(slot_idx, m * chunks))

        acc_e[...] = jnp.zeros_like(acc_e)
        some = next(f for f in (9, 3, 1) if elnode % f == 0)

        @pl.loop(0, elnode // some)
        def _(group):
            total = acc_e[...]
            for i in range(some):
                k = group * some + i
                parts = [
                    fe[s, pl.ds(c * wide + k, 1), :] for s in range(2) for c in range(3)
                ]
                total = total + contract(
                    spread(parts, row_of_entry[pl.ds(k, 1), :], own_rows), lane_hot[k]
                )
            acc_e[...] = total

        groups = plane_rows // chunks

        def home(j, m, places):
            boxes = []
            for i in places:
                q = (m * chunks + i) * per_row
                boxes.append(box_row(back, [device_at(j, q + t) for t in range(per_row)]))
            halves = split(jnp.concatenate(boxes, axis=1))
            parts = [halves[s][c : c + 1, :] for s in range(2) for c in range(3)]
            k = first_slot + j * groups + m
            lanes = slice(places[0] * LANES, (places[-1] + 1) * LANES)
            return contract(
                spread(parts, row_of_entry[k : k + 1, lanes], own_rows), lane_hot[k, :, lanes]
            )

        if per_row > 1:
            for j in range(PLANES):
                wait_first(back, j)
                wait_rest(back, j)
        total = -acc_e[...]
        for j in range(PLANES - 1, -1, -1):
            if per_row == 1:
                if j > 0:
                    wait_first(back, j)
                wait_rest(back, j)
            for m in range(groups):
                total = total + home(j, m, range(1 if j == 0 and m == 0 else 0, chunks))
        halo_wait(back)
        values = [
            jnp.concatenate([halo_side(back, 0, c), halo_side(back, 1, c)], axis=1)
            for c in range(3)
        ]
        halves = [split(-value) for value in values]
        parts = [halves[c][s] for s in range(2) for c in range(3)]
        total = total + contract(
            spread(parts, row_of_entry[lend : lend + 1, :], own_rows), lane_hot[lend]
        )
        total = total[: 3 * own_rows] + total[3 * own_rows :]
        first_acc, first_u = [], []
        for c in range(3):
            rows = slice(c * own_rows, (c + 1) * own_rows)
            first_acc.append((loads[rows, :] + total[rows]) * mass[...])
            now = cur[rows, :]
            first_u.append(2.0 * now - old[rows, :] + time_step_sq * first_acc[c])
            if step < STEPS - 1:
                old[rows, :] = now
        if per_row == 1:
            wait_first(back, 0)
        last = home(0, 0, range(1))
        last = last[: 3 * own_rows] + last[3 * own_rows :]
        for c in range(3):
            rows = slice(c * own_rows, (c + 1) * own_rows)
            change = last[rows] * mass[...]
            later = first_u[c] + time_step_sq * change
            if step == STEPS - 1:
                out_u[rows, :] = later
                out_a[rows, :] = first_acc[c] + change
            else:
                cur[rows, :] = later

    for i in range(2 * STEPS):
        box_bytes(i, n - 1, 0, 0).wait_send()
        for copy in halo_copies(i):
            copy.wait_send()


def unflatten(rows, u, a, out_u, out_a):
    for table, out in ((u, out_u), (a, out_a)):
        for c in range(3):
            for r in range(rows):
                out[c : c + 1, r * LANES : (r + 1) * LANES] = table[c * rows + r : c * rows + r + 1, :]


def on_device(
    n_py,
    displacement,
    disp_prev,
    nodal_load,
    nodal_mass,
    modulus,
    stiffness,
    connectivity,
    ghost_send,
    contact_node,
    contact_owner,
    pair_ids,
    gap_start,
    penalty,
    friction,
    slip_state,
):
    n = lax.axis_size(("px", "py"))
    cap = 2 * contact_node.shape[0] // n
    elnode, width = connectivity.shape
    nodes = displacement.shape[1]
    lent = ghost_send.shape[1]
    own_rows = nodes // LANES
    slot_rows = n * cap // LANES
    wide = -(-elnode // SUBLANES) * SUBLANES
    pair_rows = pair_ids.shape[1] // LANES
    slot_groups = slot_rows * LANES // width
    pair_groups = pair_ids.shape[1] // width
    inner = width * 3 // 4
    entries = elnode + 1 + 2 * pair_groups + slot_groups
    flat = (3 * own_rows, LANES)
    vmem = pl.BlockSpec(memory_space=pltpu.VMEM)
    hbm = pl.BlockSpec(memory_space=pltpu.HBM)
    f32, bf16, i32 = jnp.float32, jnp.bfloat16, jnp.int32
    dma = pltpu.SemaphoreType.DMA
    args = [
        displacement,
        disp_prev,
        nodal_load,
        nodal_mass.reshape(-1, LANES),
        modulus.reshape(1, -1),
        stiffness,
        connectivity,
        ghost_send,
        contact_node.reshape(-1, LANES),
        contact_owner.reshape(-1, LANES),
        pair_ids,
        gap_start,
        penalty.reshape(-1, LANES),
        friction.reshape(-1, LANES),
        slip_state,
    ]
    new_u, acc = pl.pallas_call(
        functools.partial(kernel, (n_py, n, cap, elnode, lent, width, inner)),
        out_shape=[jax.ShapeDtypeStruct(flat, f32)] * 2,
        in_specs=[hbm] * len(args),
        out_specs=[vmem] * 2,
        scratch_shapes=[pltpu.VMEM(a.shape, a.dtype) for a in args]
        + [
            pltpu.VMEM((entries, width), i32),
            pltpu.VMEM((entries, LANES, width), bf16),
            pltpu.VMEM((3 * wide, 9 * wide), f32),
            pltpu.VMEM((slot_rows, LANES), i32),
            pltpu.VMEM((2 * pair_rows, LANES), i32),
            pltpu.VMEM((SUBLANES, LANES), i32),
            pltpu.VMEM((3 * wide, width), f32),
            pltpu.VMEM((2, 3 * wide, width), f32),
            pltpu.VMEM((6 * own_rows, LANES), f32),
            pltpu.VMEM(flat, f32),
            pltpu.VMEM(flat, f32),
            pltpu.VMEM(flat, f32),
            pltpu.VMEM((3 * pair_rows, LANES), f32),
            pltpu.VMEM((3 * pair_rows, LANES), i32),
            pltpu.VMEM((2 * STEPS, n, 3, cap), f32),
            pltpu.VMEM((2 * STEPS, n, 3, cap), f32),
            pltpu.VMEM((2 * STEPS, 2, 3, lent), f32),
            pltpu.VMEM((2 * STEPS, 2, 3, lent), f32),
            dma((len(args),)),
            dma((2 * STEPS,)),
            dma((2 * STEPS, PLANES, 2)),
            dma((2 * STEPS, 2)),
            dma((2 * STEPS, 2)),
        ],
        compiler_params=pltpu.CompilerParams(
            collective_id=0, has_side_effects=True, vmem_limit_bytes=67043328
        ),
        name="contact_steps",
    )(*args)
    return pl.pallas_call(
        functools.partial(unflatten, own_rows),
        out_shape=[jax.ShapeDtypeStruct(displacement.shape, f32)] * 2,
        in_specs=[vmem] * 2,
        out_specs=[vmem] * 2,
        name="unflatten",
    )(new_u, acc)


def solution(mesh):
    both = ("px", "py")
    row, cols = P(both), P(None, both)
    return jax.shard_map(
        functools.partial(on_device, mesh.shape["py"]),
        mesh=mesh,
        in_specs=(cols, cols, cols, row, row, P(), cols, cols, row, row, cols, cols, row, row, cols),
        out_specs=(cols, cols),
        check_vma=False,
    )
```

```python
import functools

import jax
import jax.numpy as jnp
from jax import lax
from jax.experimental import pallas as pl
from jax.experimental.pallas import tpu as pltpu
from jax.sharding import PartitionSpec as P

STEPS = 3
LANES = 128
SUBLANES = 8
PLANES = 4
KINDS = 2
MESH = pl.DeviceIdType.MESH

time_step_sq = 0.05


def matches(index_row, rows):
    return lax.broadcasted_iota(jnp.int32, (rows, index_row.shape[1]), 0) == index_row


def split(value):
    high = value.astype(jnp.bfloat16).astype(jnp.float32)
    return high, value - high


def contract(left, right):
    return lax.dot_general(
        left, right, (((1,), (1,)), ((), ())), preferred_element_type=jnp.float32
    )


def spread(parts, row_index, rows):
    mask = matches(row_index, rows)
    return jnp.concatenate([jnp.where(mask, part, 0.0) for part in parts], axis=0).astype(
        jnp.bfloat16
    )


def pick(got, lines, row_of, lane_of, r):
    mask = row_of == r
    for c in range(3):
        line = jnp.broadcast_to(lines[c], (SUBLANES, LANES))
        value = jnp.take_along_axis(line, lane_of, axis=1, mode="promise_in_bounds")
        got[c] = jnp.where(mask, value, got[c])


def blank():
    return [jnp.zeros((SUBLANES, LANES), jnp.float32)] * 3


def places_of(index):
    return lax.shift_right_arithmetic(index, 7), index & (LANES - 1)


def kernel(
    dims,
    disp_hbm,
    prev_hbm,
    load_hbm,
    mass_hbm,
    mod_hbm,
    stiff_hbm,
    conn_hbm,
    ghost_hbm,
    node_hbm,
    owner_hbm,
    pair_hbm,
    gap_hbm,
    pen_hbm,
    fric_hbm,
    slip_hbm,
    out_u,
    out_a,
    disp,
    prev,
    load,
    mass,
    mod,
    stiff,
    conn,
    ghost,
    node,
    owner,
    pair,
    gap0,
    pen,
    fric,
    slip,
    row_of_entry,
    lane_hot,
    stiff_parts,
    slot_idx,
    pair_idx,
    lend_idx,
    ue,
    fe,
    acc_e,
    cur,
    old,
    loads,
    gaps,
    slips,
    box_out,
    box_in,
    halo_out,
    halo_in,
    in_sem,
    box_send,
    box_recv,
    halo_send,
    halo_recv,
):
    n_py, n, cap, elnode, lent, width, inner = dims
    px, py = lax.axis_index("px"), lax.axis_index("py")
    me = px * n_py + py

    def place(device):
        return {"px": lax.div(device, n_py), "py": lax.rem(device, n_py)}

    fills = [
        pltpu.make_async_copy(source, target, in_sem.at[i])
        for i, (source, target) in enumerate(
            [
                (owner_hbm, owner),
                (node_hbm, node),
                (disp_hbm, disp),
                (ghost_hbm, ghost),
                (conn_hbm, conn),
                (pair_hbm, pair),
                (stiff_hbm, stiff),
                (mod_hbm, mod),
                (gap_hbm, gap0),
                (slip_hbm, slip),
                (pen_hbm, pen),
                (fric_hbm, fric),
                (prev_hbm, prev),
                (load_hbm, load),
                (mass_hbm, mass),
            ]
        )
    ]
    for fill in fills:
        fill.start()

    barrier = pltpu.get_barrier_semaphore()

    @pl.loop(1, n)
    def _(d):
        pl.semaphore_signal(
            barrier, inc=1, device_id=place(lax.rem(me + d, n)), device_id_type=MESH
        )

    per_plane = n // PLANES
    rows_y = n_py // PLANES
    rows_x = n // n_py // 2
    z, y = lax.div(py, rows_y), lax.rem(py, rows_y)
    x, core = lax.div(px, 2), lax.rem(px, 2)
    plane_at = [PLANES - 1 - z, lax.rem(z + 2, PLANES), z + 1 - 2 * lax.rem(z, 2), z]
    planes = [plane * rows_y for plane in plane_at]
    turns = [(a, e, b) for a in range(rows_x) for e in range(2) for b in range(rows_y)]
    columns = [
        (lax.rem(x + a, rows_x) * 2 + lax.rem(core + e, 2), lax.rem(y + b, rows_y))
        for a, e, b in turns
    ]

    def hops(place):
        j, (a, e, b) = place[0], turns[place[1]]
        return PLANES - 1 - j + min(a, rows_x - a) + min(b, rows_y - b) + 1 - e

    places = sorted(
        [(j, t) for j in range(PLANES) for t in range(per_plane)], key=hops, reverse=True
    )
    kinds = [0 if hops(place) > hops(places[0]) - 2 else 1 for place in places]
    my_p = places.index((PLANES - 1, 0))
    members = [[p for p in range(n) if kinds[p] == kind] for kind in range(KINDS)]

    def place_at(p):
        j, t = places[p]
        return {"px": columns[t][0], "py": columns[t][1] + planes[j]}

    def device_at(p):
        there = place_at(p)
        return there["px"] * n_py + there["py"]

    own_rows = cur.shape[0] // 3
    slot_rows = slot_idx.shape[0]
    plane_rows = slot_rows // PLANES
    per_row = LANES // cap
    wide = ue.shape[0] // 3
    lent_rows = lent // LANES
    ghost_rows = 2 * lent_rows
    chunks = width // LANES
    pair_rows = pair_idx.shape[0] // 2
    pair_groups = pair_rows // chunks
    slot_groups = slot_rows // chunks
    lend = elnode
    near, far = lend + 1, lend + 1 + pair_groups
    first_slot = far + pair_groups

    def set_row(k, row):
        row_of_entry[pl.ds(k, 1), :] = lax.shift_right_arithmetic(row, 7)
        lane_hot[k] = jnp.where(matches(row & (LANES - 1), LANES), 1.0, 0.0).astype(jnp.bfloat16)

    def flat_row(table, first):
        return jnp.concatenate([table[first + i : first + i + 1, :] for i in range(chunks)], axis=1)

    for fill in fills[:2]:
        fill.wait()

    from_lane = lax.broadcasted_iota(jnp.int32, (LANES, 2 * LANES), 0)
    to_lane = lax.broadcasted_iota(jnp.int32, (LANES, 2 * LANES), 1)
    before = jnp.where(from_lane < to_lane, 1.0, 0.0).astype(jnp.bfloat16)
    target = owner[...]
    target_py = lax.rem(target, n_py)
    target_z = lax.div(target_py, rows_y)
    target_j = jnp.where(
        target_z == plane_at[0],
        0,
        jnp.where(target_z == plane_at[1], 1, jnp.where(target_z == plane_at[2], 2, 3)),
    )
    target_px = lax.div(target, n_py)
    a = lax.rem(lax.div(target_px, 2) - x + rows_x, rows_x)
    e = lax.rem(lax.rem(target_px, 2) - core + 2, 2)
    b = lax.rem(lax.rem(target_py, rows_y) - y + rows_y, rows_y)
    turn = target_j * per_plane + (a * 2 + e) * rows_y + b
    spot = jnp.zeros_like(target)
    for p, (j, t) in enumerate(places):
        spot = jnp.where(turn == j * per_plane + t, p, spot)
    pieces = owner.shape[0]
    hot = [jnp.where(matches(spot[i : i + 1, :], n), 1.0, 0.0) for i in range(pieces)]
    counts = jnp.dot(
        jnp.concatenate(hot, axis=0).astype(jnp.bfloat16),
        before,
        preferred_element_type=jnp.float32,
    )
    carry = jnp.zeros((n, LANES), jnp.float32)
    ranks = []
    for i in range(pieces):
        earlier = counts[i * n : (i + 1) * n, :LANES]
        ranks.append(jnp.sum(hot[i] * (earlier + carry), axis=0, keepdims=True))
        carry = carry + counts[i * n : (i + 1) * n, LANES:]
    found = jnp.zeros((2 * slot_rows, LANES), jnp.float32)
    for first in range(0, pieces, chunks):
        lefts, rights = [], []
        for i in range(first, first + chunks):
            number = node[i : i + 1, :] + 1
            slot = spot[i : i + 1, :] * cap + ranks[i].astype(jnp.int32)
            parts = [
                lax.shift_right_arithmetic(number, 6).astype(jnp.float32),
                (number & 63).astype(jnp.float32),
            ]
            lefts.append(spread(parts, lax.shift_right_arithmetic(slot, 7), slot_rows))
            rights.append(
                jnp.where(matches(slot & (LANES - 1), LANES), 1.0, 0.0).astype(jnp.bfloat16)
            )
        found = found + contract(
            jnp.concatenate(lefts, axis=1), jnp.concatenate(rights, axis=1)
        )
    slot_idx[...] = (found[:slot_rows] * 64.0 + found[slot_rows:]).astype(jnp.int32) - 1

    for fill in fills[2:4]:
        fill.wait()

    def to_rows(table, source, rows):
        for c in range(3):
            for r in range(rows):
                table[c * rows + r : c * rows + r + 1, :] = source[
                    c : c + 1, r * LANES : (r + 1) * LANES
                ]

    to_rows(cur, disp, own_rows)
    lend_idx[...] = jnp.full_like(lend_idx, -1)
    for side in range(2):
        for r in range(lent_rows):
            at = side * lent_rows + r
            lend_idx[at : at + 1, :] = ghost[side : side + 1, r * LANES : (r + 1) * LANES]

    def box_copy(i, p, spot_out):
        return pltpu.make_async_remote_copy(
            src_ref=box_out.at[i, spot_out],
            dst_ref=box_in.at[i, me],
            send_sem=box_send.at[i],
            recv_sem=box_recv.at[i, kinds[p]],
            device_id=place_at(p),
            device_id_type=MESH,
        )

    def box_bytes(i, count, kind):
        every = pl.ds(0, count)
        return pltpu.make_async_remote_copy(
            src_ref=box_out.at[i, every],
            dst_ref=box_in.at[i, every],
            send_sem=box_send.at[i],
            recv_sem=box_recv.at[i, kind],
            device_id=place(lax.rem(me + 1, n)),
            device_id_type=MESH,
        )

    def box_start(i, spots, by_device):
        for p in spots:
            if p != my_p:
                box_copy(i, p, device_at(p) if by_device else p).start()

    def box_wait(i, kind):
        box_bytes(i, len([p for p in members[kind] if p != my_p]), kind).wait_recv()

    def halo_copies(i):
        copies = []
        for side, step in ((0, n - 1), (1, 1)):
            copies.append(
                pltpu.make_async_remote_copy(
                    src_ref=halo_out.at[i, side],
                    dst_ref=halo_in.at[i, 1 - side],
                    send_sem=halo_send.at[i, side],
                    recv_sem=halo_recv.at[i, 1 - side],
                    device_id=place(lax.rem(me + step, n)),
                    device_id_type=MESH,
                )
            )
        return copies

    def halo_start(i):
        for copy in halo_copies(i):
            copy.start()

    def halo_wait(i):
        for copy in halo_copies(i):
            copy.wait_recv()

    def halo_side(i, side, c):
        inside = me > 0 if side == 0 else me < n - 1
        return jnp.where(inside, halo_in[i, side, c : c + 1, :], 0.0)

    def box_row(i, devices):
        boxes = [box_in[i, device] for device in devices]
        return boxes[0] if per_row == 1 else jnp.concatenate(boxes, axis=1)

    def table_lines(table, rows, r):
        return [table[c * rows + r : c * rows + r + 1, :] for c in range(3)]

    for step in range(STEPS):
        going, back = 2 * step, 2 * step + 1

        def send_block(table, slots, j):
            row_of, lane_of = places_of(slots[j * SUBLANES : (j + 1) * SUBLANES, :])
            got = blank()
            for r in range(own_rows):
                pick(got, table_lines(table, own_rows, r), row_of, lane_of, r)
            spots = range(j * SUBLANES * per_row, (j + 1) * SUBLANES * per_row)
            for p in spots:
                r, l = divmod(p * cap - j * SUBLANES * LANES, LANES)
                for c in range(3):
                    box_out[going, p, c : c + 1, :] = got[c][r : r + 1, l : l + cap]
            if step == 0 and j == 0:
                pl.semaphore_wait(barrier, n - 1)
            box_start(going, spots, False)

        send_block(cur, slot_idx, 0)
        now_at = cur[...]
        slots = slot_idx[...]
        lent_at = places_of(lend_idx[...])
        for j in range(1, slot_rows // SUBLANES):
            send_block(now_at, slots, j)
        got = blank()
        for r in range(own_rows):
            pick(got, table_lines(now_at, own_rows, r), *lent_at, r)
        for c in range(3):
            for side in range(2):
                for r in range(lent_rows):
                    at = side * lent_rows + r
                    halo_out[going, side, c : c + 1, r * LANES : (r + 1) * LANES] = got[c][
                        at : at + 1
                    ]
        halo_start(going)
        box_in[going, me] = box_out[going, my_p]

        if step == 0:
            for fill in fills[4:]:
                fill.wait()

            @pl.loop(0, elnode)
            def _(k):
                set_row(k, conn[pl.ds(k, 1), :])

            for i in range(2):
                for r in range(pair_rows):
                    pair_idx[i * pair_rows + r : i * pair_rows + r + 1, :] = pair[
                        i : i + 1, r * LANES : (r + 1) * LANES
                    ]
            for i, first in ((0, near), (1, far)):
                for h in range(pair_groups):
                    set_row(first + h, pair[i : i + 1, h * width : (h + 1) * width])
            set_row(lend, flat_row(lend_idx, 0))
            to_rows(gaps, gap0, pair_rows)
            to_rows(slips, slip, pair_rows)
            to_rows(old, prev, own_rows)
            to_rows(loads, load, own_rows)
            mass[...] = 1.0 / mass[...]
            ue[...] = jnp.zeros_like(ue)
            stiff_parts[...] = jnp.zeros_like(stiff_parts)
            for c in range(3):
                for d in range(3):
                    block = stiff[c * elnode : (c + 1) * elnode, d * elnode : (d + 1) * elnode]
                    high, low = split(block)
                    for at, part in ((0, high), (1, high), (2, low)):
                        start = (3 * at + d) * wide
                        stiff_parts[c * wide : c * wide + elnode, start : start + elnode] = part

        def forces(cols):
            high, low = split(ue[:, cols])
            right = jnp.concatenate([high, low, high], axis=0).astype(jnp.bfloat16)
            left = stiff_parts[...].astype(jnp.bfloat16)
            product = jnp.dot(left, right, preferred_element_type=jnp.float32) * mod[:, cols]
            high, low = split(product)
            fe[0, :, cols] = high
            fe[1, :, cols] = low

        tops = [min(k, elnode - SUBLANES) for k in range(0, elnode, SUBLANES)]

        @pl.loop(0, chunks)
        def _(i):
            lanes = pl.ds(pl.multiple_of(i * LANES, LANES), LANES)
            for top in tops:
                row_of, lane_of = places_of(conn[top : top + SUBLANES, lanes])
                got = blank()
                for r in range(own_rows):
                    pick(got, table_lines(cur, own_rows, r), row_of, lane_of, r)
                for c in range(3):
                    ue[c * wide + top : c * wide + top + SUBLANES, lanes] = got[c]

        forces(slice(0, inner))

        pair_at = [places_of(pair_idx[i * pair_rows : (i + 1) * pair_rows, :]) for i in range(2)]
        ends = [blank(), blank()]

        def pair_pick(lines_of, row):
            for i in range(2):
                pick(ends[i], lines_of, *pair_at[i], row)

        def pair_picks(kind):
            box_wait(going, kind)
            for p in members[kind]:
                there = device_at(p)
                pair_pick([box_in[going, there, c : c + 1, :] for c in range(3)], there)

        if per_row == 1:
            for kind in range(KINDS - 1, 0, -1):
                pair_picks(kind)

        if per_row == 1:
            pair_picks(0)
        else:
            for kind in range(KINDS):
                box_wait(going, kind)
            for r in range(slot_rows):
                box = box_row(going, [r * per_row + t for t in range(per_row)])
                pair_pick([box[c : c + 1, :] for c in range(3)], r)
        gap = [
            gaps[c * pair_rows : (c + 1) * pair_rows, :] + ends[1][c] - ends[0][c] for c in range(3)
        ]
        normal = pen[...] * jnp.maximum(-gap[2], 0.0)
        length = jnp.sqrt(gap[0] * gap[0] + gap[1] * gap[1] + 0.01)
        slipping = slips[step * pair_rows : (step + 1) * pair_rows, :] == 1
        factor = jnp.where(slipping, -fric[...] * normal / length, -0.5 * pen[...])
        force = [factor * gap[0], factor * gap[1], normal]
        halves = [split(value) for value in force]
        total = jnp.zeros((6 * slot_rows, LANES), jnp.float32)
        for sign, first in ((1.0, far), (-1.0, near)):
            for h in range(pair_groups):
                parts = [
                    flat_row(sign * halves[c][s], h * chunks) for s in range(2) for c in range(3)
                ]
                k = first + h
                total = total + contract(
                    spread(parts, row_of_entry[k : k + 1, :], slot_rows), lane_hot[k]
                )
        total = total[: 3 * slot_rows] + total[3 * slot_rows :]
        for g in range(n):
            r, l = divmod(g * cap, LANES)
            for c in range(3):
                at = c * slot_rows + r
                box_out[back, g, c : c + 1, :] = total[at : at + 1, l : l + cap]
        box_start(back, range(n), True)
        box_in[back, me] = box_out[back, me]

        halo_wait(going)
        ghosts = [[halo_side(going, side, c) for c in range(3)] for side in range(2)]
        for top in tops:
            row_of, lane_of = places_of(conn[top : top + SUBLANES, inner:])
            for b in range((width - inner) // LANES):
                lanes = slice(b * LANES, (b + 1) * LANES)
                spots = slice(inner + b * LANES, inner + (b + 1) * LANES)
                got = [ue[c * wide + top : c * wide + top + SUBLANES, spots] for c in range(3)]
                for side in range(2):
                    for r in range(lent_rows):
                        lines = [
                            ghosts[side][c][:, r * LANES : (r + 1) * LANES] for c in range(3)
                        ]
                        at = own_rows + side * lent_rows + r
                        pick(got, lines, row_of[:, lanes], lane_of[:, lanes], at)
                for c in range(3):
                    ue[c * wide + top : c * wide + top + SUBLANES, spots] = got[c]
        forces(slice(inner, width))

        edge = jnp.zeros((6 * ghost_rows, LANES), jnp.float32)
        for first in range(0, elnode, chunks):
            lefts, rights = [], []
            for k in range(first, min(first + chunks, elnode)):
                row = row_of_entry[k : k + 1, inner:] - own_rows
                parts = [
                    fe[s, c * wide + k : c * wide + k + 1, inner:] for s in range(2) for c in range(3)
                ]
                lefts.append(spread(parts, row, ghost_rows))
                rights.append(lane_hot[k, :, inner:])
            edge = edge + contract(
                jnp.concatenate(lefts, axis=1), jnp.concatenate(rights, axis=1)
            )
        edge = edge[: 3 * ghost_rows] + edge[3 * ghost_rows :]
        for c in range(3):
            for side in range(2):
                for r in range(lent_rows):
                    at = c * ghost_rows + side * lent_rows + r
                    halo_out[back, side, c : c + 1, r * LANES : (r + 1) * LANES] = edge[at : at + 1]
        halo_start(back)

        if step == 0:
            for m in range(slot_groups):
                set_row(first_slot + m, flat_row(slot_idx, m * chunks))

        acc_e[...] = jnp.zeros_like(acc_e)
        some = next(f for f in (9, 3, 1) if elnode % f == 0)

        @pl.loop(0, elnode // some)
        def _(group):
            total = acc_e[...]
            for i in range(some):
                k = group * some + i
                parts = [
                    fe[s, pl.ds(c * wide + k, 1), :] for s in range(2) for c in range(3)
                ]
                total = total + contract(
                    spread(parts, row_of_entry[pl.ds(k, 1), :], own_rows), lane_hot[k]
                )
            acc_e[...] = total

        def home(rows):
            lefts, rights = [], []
            for at in range(0, len(rows), chunks):
                boxes, spots, hots = [], [], []
                for r in rows[at : at + chunks]:
                    k, l = first_slot + r // chunks, r % chunks * LANES
                    boxes.append(
                        box_row(back, [device_at(r * per_row + t) for t in range(per_row)])
                    )
                    spots.append(row_of_entry[k : k + 1, l : l + LANES])
                    hots.append(lane_hot[k, :, l : l + LANES])
                halves = split(jnp.concatenate(boxes, axis=1))
                parts = [halves[s][c : c + 1, :] for s in range(2) for c in range(3)]
                lefts.append(spread(parts, jnp.concatenate(spots, axis=1), own_rows))
                rights.append(jnp.concatenate(hots, axis=1))
            return lefts, rights

        def gathered(lefts, rights):
            return contract(jnp.concatenate(lefts, axis=1), jnp.concatenate(rights, axis=1))

        if per_row == 1:
            start = -(-members[1][0] // chunks) * chunks
            early, late = [*range(start, n), *range(members[1][0], start)], members[0]
        else:
            early, late = range(slot_rows - plane_rows, slot_rows), range(slot_rows - plane_rows)
            box_wait(back, 0)
        box_wait(back, 1)
        total = -acc_e[...]
        lefts, rights = home(early)
        for left, right in zip(lefts, rights):
            total = total + contract(left, right)
        total = total[: 3 * own_rows] + total[3 * own_rows :]
        first_acc, first_u = [], []
        for c in range(3):
            rows = slice(c * own_rows, (c + 1) * own_rows)
            first_acc.append((loads[rows, :] + total[rows]) * mass[...])
            now = cur[rows, :]
            first_u.append(2.0 * now - old[rows, :] + time_step_sq * first_acc[c])
            if step < STEPS - 1:
                old[rows, :] = now
        if per_row == 1:
            box_wait(back, 0)
        halo_wait(back)
        lefts, rights = home(late)
        values = [
            jnp.concatenate([halo_side(back, 0, c), halo_side(back, 1, c)], axis=1)
            for c in range(3)
        ]
        halves = [split(-value) for value in values]
        parts = [halves[c][s] for s in range(2) for c in range(3)]
        lefts.append(spread(parts, row_of_entry[lend : lend + 1, :], own_rows))
        rights.append(lane_hot[lend])
        last = gathered(lefts, rights)
        last = last[: 3 * own_rows] + last[3 * own_rows :]
        for c in range(3):
            rows = slice(c * own_rows, (c + 1) * own_rows)
            change = last[rows] * mass[...]
            later = first_u[c] + time_step_sq * change
            if step == STEPS - 1:
                out_u[rows, :] = later
                out_a[rows, :] = first_acc[c] + change
            else:
                cur[rows, :] = later

    for i in range(2 * STEPS):
        box_bytes(i, n - 1, 0).wait_send()
        for copy in halo_copies(i):
            copy.wait_send()


def unflatten(rows, u, a, out_u, out_a):
    for table, out in ((u, out_u), (a, out_a)):
        for c in range(3):
            for r in range(rows):
                out[c : c + 1, r * LANES : (r + 1) * LANES] = table[c * rows + r : c * rows + r + 1, :]


def on_device(
    n_py,
    displacement,
    disp_prev,
    nodal_load,
    nodal_mass,
    modulus,
    stiffness,
    connectivity,
    ghost_send,
    contact_node,
    contact_owner,
    pair_ids,
    gap_start,
    penalty,
    friction,
    slip_state,
):
    n = lax.axis_size(("px", "py"))
    cap = 2 * contact_node.shape[0] // n
    elnode, width = connectivity.shape
    nodes = displacement.shape[1]
    lent = ghost_send.shape[1]
    own_rows = nodes // LANES
    slot_rows = n * cap // LANES
    wide = -(-elnode // SUBLANES) * SUBLANES
    pair_rows = pair_ids.shape[1] // LANES
    slot_groups = slot_rows * LANES // width
    pair_groups = pair_ids.shape[1] // width
    inner = width * 3 // 4
    entries = elnode + 1 + 2 * pair_groups + slot_groups
    flat = (3 * own_rows, LANES)
    vmem = pl.BlockSpec(memory_space=pltpu.VMEM)
    hbm = pl.BlockSpec(memory_space=pltpu.HBM)
    f32, bf16, i32 = jnp.float32, jnp.bfloat16, jnp.int32
    dma = pltpu.SemaphoreType.DMA
    args = [
        displacement,
        disp_prev,
        nodal_load,
        nodal_mass.reshape(-1, LANES),
        modulus.reshape(1, -1),
        stiffness,
        connectivity,
        ghost_send,
        contact_node.reshape(-1, LANES),
        contact_owner.reshape(-1, LANES),
        pair_ids,
        gap_start,
        penalty.reshape(-1, LANES),
        friction.reshape(-1, LANES),
        slip_state,
    ]
    new_u, acc = pl.pallas_call(
        functools.partial(kernel, (n_py, n, cap, elnode, lent, width, inner)),
        out_shape=[jax.ShapeDtypeStruct(flat, f32)] * 2,
        in_specs=[hbm] * len(args),
        out_specs=[vmem] * 2,
        scratch_shapes=[pltpu.VMEM(a.shape, a.dtype) for a in args]
        + [
            pltpu.VMEM((entries, width), i32),
            pltpu.VMEM((entries, LANES, width), bf16),
            pltpu.VMEM((3 * wide, 9 * wide), f32),
            pltpu.VMEM((slot_rows, LANES), i32),
            pltpu.VMEM((2 * pair_rows, LANES), i32),
            pltpu.VMEM((SUBLANES, LANES), i32),
            pltpu.VMEM((3 * wide, width), f32),
            pltpu.VMEM((2, 3 * wide, width), f32),
            pltpu.VMEM((6 * own_rows, LANES), f32),
            pltpu.VMEM(flat, f32),
            pltpu.VMEM(flat, f32),
            pltpu.VMEM(flat, f32),
            pltpu.VMEM((3 * pair_rows, LANES), f32),
            pltpu.VMEM((3 * pair_rows, LANES), i32),
            pltpu.VMEM((2 * STEPS, n, 3, cap), f32),
            pltpu.VMEM((2 * STEPS, n, 3, cap), f32),
            pltpu.VMEM((2 * STEPS, 2, 3, lent), f32),
            pltpu.VMEM((2 * STEPS, 2, 3, lent), f32),
            dma((len(args),)),
            dma((2 * STEPS,)),
            dma((2 * STEPS, KINDS)),
            dma((2 * STEPS, 2)),
            dma((2 * STEPS, 2)),
        ],
        compiler_params=pltpu.CompilerParams(
            collective_id=0, has_side_effects=True, vmem_limit_bytes=67043328
        ),
        name="contact_steps",
    )(*args)
    return pl.pallas_call(
        functools.partial(unflatten, own_rows),
        out_shape=[jax.ShapeDtypeStruct(displacement.shape, f32)] * 2,
        in_specs=[vmem] * 2,
        out_specs=[vmem] * 2,
        name="unflatten",
    )(new_u, acc)


def solution(mesh):
    both = ("px", "py")
    row, cols = P(both), P(None, both)
    return jax.shard_map(
        functools.partial(on_device, mesh.shape["py"]),
        mesh=mesh,
        in_specs=(cols, cols, cols, row, row, P(), cols, cols, row, row, cols, cols, row, row, cols),
        out_specs=(cols, cols),
        check_vma=False,
    )
```

```python
import functools

import jax
import jax.numpy as jnp
from jax import lax
from jax.experimental import pallas as pl
from jax.experimental.pallas import tpu as pltpu
from jax.sharding import PartitionSpec as P

STEPS = 3
LANES = 128
SUBLANES = 8
PLANES = 4
KINDS = 2
MESH = pl.DeviceIdType.MESH

time_step_sq = 0.05


def matches(index_row, rows):
    return lax.broadcasted_iota(jnp.int32, (rows, index_row.shape[1]), 0) == index_row


def split(value):
    high = value.astype(jnp.bfloat16).astype(jnp.float32)
    return high, value - high


def contract(left, right):
    return lax.dot_general(
        left, right, (((1,), (1,)), ((), ())), preferred_element_type=jnp.float32
    )


def spread(parts, row_index, rows):
    mask = matches(row_index, rows)
    return jnp.concatenate([jnp.where(mask, part, 0.0) for part in parts], axis=0).astype(
        jnp.bfloat16
    )


def pick(got, lines, row_of, lane_of, r):
    mask = row_of == r
    for c in range(3):
        line = jnp.broadcast_to(lines[c], (SUBLANES, LANES))
        value = jnp.take_along_axis(line, lane_of, axis=1, mode="promise_in_bounds")
        got[c] = jnp.where(mask, value, got[c])


def blank():
    return [jnp.zeros((SUBLANES, LANES), jnp.float32)] * 3


def places_of(index):
    return lax.shift_right_arithmetic(index, 7), index & (LANES - 1)


def kernel(
    dims,
    disp_hbm,
    prev_hbm,
    load_hbm,
    mass_hbm,
    mod_hbm,
    stiff_hbm,
    conn_hbm,
    ghost_hbm,
    node_hbm,
    owner_hbm,
    pair_hbm,
    gap_hbm,
    pen_hbm,
    fric_hbm,
    slip_hbm,
    out_u,
    out_a,
    disp,
    prev,
    load,
    mass,
    mod,
    stiff,
    conn,
    ghost,
    node,
    owner,
    pair,
    gap0,
    pen,
    fric,
    slip,
    row_of_entry,
    lane_hot,
    stiff_parts,
    slot_idx,
    pair_idx,
    lend_idx,
    ue,
    fe,
    acc_e,
    cur,
    old,
    loads,
    gaps,
    slips,
    box_out,
    box_in,
    halo_out,
    halo_in,
    in_sem,
    box_send,
    box_recv,
    halo_send,
    halo_recv,
):
    n_py, n, cap, elnode, lent, width, inner = dims
    px, py = lax.axis_index("px"), lax.axis_index("py")
    me = px * n_py + py

    def place(device):
        return {"px": lax.div(device, n_py), "py": lax.rem(device, n_py)}

    fills = [
        pltpu.make_async_copy(source, target, in_sem.at[i])
        for i, (source, target) in enumerate(
            [
                (owner_hbm, owner),
                (node_hbm, node),
                (disp_hbm, disp),
                (ghost_hbm, ghost),
                (conn_hbm, conn),
                (pair_hbm, pair),
                (stiff_hbm, stiff),
                (mod_hbm, mod),
                (gap_hbm, gap0),
                (slip_hbm, slip),
                (pen_hbm, pen),
                (fric_hbm, fric),
                (prev_hbm, prev),
                (load_hbm, load),
                (mass_hbm, mass),
            ]
        )
    ]
    for fill in fills:
        fill.start()

    barrier = pltpu.get_barrier_semaphore()

    @pl.loop(1, n)
    def _(d):
        pl.semaphore_signal(
            barrier, inc=1, device_id=place(lax.rem(me + d, n)), device_id_type=MESH
        )

    per_plane = n // PLANES
    rows_y = n_py // PLANES
    rows_x = n // n_py // 2
    z, y = lax.div(py, rows_y), lax.rem(py, rows_y)
    x, core = lax.div(px, 2), lax.rem(px, 2)
    plane_at = [PLANES - 1 - z, lax.rem(z + 2, PLANES), z + 1 - 2 * lax.rem(z, 2), z]
    planes = [plane * rows_y for plane in plane_at]
    turns = [(a, e, b) for a in range(rows_x) for e in range(2) for b in range(rows_y)]
    columns = [
        (lax.rem(x + a, rows_x) * 2 + lax.rem(core + e, 2), lax.rem(y + b, rows_y))
        for a, e, b in turns
    ]

    def hops(place):
        j, (a, e, b) = place[0], turns[place[1]]
        return PLANES - 1 - j + min(a, rows_x - a) + min(b, rows_y - b) + 1 - e

    places = sorted(
        [(j, t) for j in range(PLANES) for t in range(per_plane)], key=hops, reverse=True
    )
    kinds = [0 if hops(place) > hops(places[0]) - 2 else 1 for place in places]
    my_p = places.index((PLANES - 1, 0))
    members = [[p for p in range(n) if kinds[p] == kind] for kind in range(KINDS)]

    def place_at(p):
        j, t = places[p]
        return {"px": columns[t][0], "py": columns[t][1] + planes[j]}

    def device_at(p):
        there = place_at(p)
        return there["px"] * n_py + there["py"]

    own_rows = cur.shape[0] // 3
    slot_rows = slot_idx.shape[0]
    plane_rows = slot_rows // PLANES
    per_row = LANES // cap
    wide = ue.shape[0] // 3
    lent_rows = lent // LANES
    ghost_rows = 2 * lent_rows
    chunks = width // LANES
    pair_rows = pair_idx.shape[0] // 2
    pair_groups = pair_rows // chunks
    slot_groups = slot_rows // chunks
    lend = elnode
    near, far = lend + 1, lend + 1 + pair_groups
    first_slot = far + pair_groups

    def set_row(k, row):
        row_of_entry[pl.ds(k, 1), :] = lax.shift_right_arithmetic(row, 7)
        lane_hot[k] = jnp.where(matches(row & (LANES - 1), LANES), 1.0, 0.0).astype(jnp.bfloat16)

    def flat_row(table, first):
        return jnp.concatenate([table[first + i : first + i + 1, :] for i in range(chunks)], axis=1)

    for fill in fills[:2]:
        fill.wait()

    from_lane = lax.broadcasted_iota(jnp.int32, (LANES, 2 * LANES), 0)
    to_lane = lax.broadcasted_iota(jnp.int32, (LANES, 2 * LANES), 1)
    before = jnp.where(from_lane < to_lane, 1.0, 0.0).astype(jnp.bfloat16)
    target = owner[...]
    target_py = lax.rem(target, n_py)
    target_z = lax.div(target_py, rows_y)
    target_j = jnp.where(
        target_z == plane_at[0],
        0,
        jnp.where(target_z == plane_at[1], 1, jnp.where(target_z == plane_at[2], 2, 3)),
    )
    target_px = lax.div(target, n_py)
    a = lax.rem(lax.div(target_px, 2) - x + rows_x, rows_x)
    e = lax.rem(lax.rem(target_px, 2) - core + 2, 2)
    b = lax.rem(lax.rem(target_py, rows_y) - y + rows_y, rows_y)
    turn = target_j * per_plane + (a * 2 + e) * rows_y + b
    spot = jnp.zeros_like(target)
    for p, (j, t) in enumerate(places):
        spot = jnp.where(turn == j * per_plane + t, p, spot)
    pieces = owner.shape[0]
    hot = [jnp.where(matches(spot[i : i + 1, :], n), 1.0, 0.0) for i in range(pieces)]
    counts = jnp.dot(
        jnp.concatenate(hot, axis=0).astype(jnp.bfloat16),
        before,
        preferred_element_type=jnp.float32,
    )
    carry = jnp.zeros((n, LANES), jnp.float32)
    ranks = []
    for i in range(pieces):
        earlier = counts[i * n : (i + 1) * n, :LANES]
        ranks.append(jnp.sum(hot[i] * (earlier + carry), axis=0, keepdims=True))
        carry = carry + counts[i * n : (i + 1) * n, LANES:]
    found = jnp.zeros((2 * slot_rows, LANES), jnp.float32)
    for first in range(0, pieces, chunks):
        lefts, rights = [], []
        for i in range(first, first + chunks):
            number = node[i : i + 1, :] + 1
            slot = spot[i : i + 1, :] * cap + ranks[i].astype(jnp.int32)
            parts = [
                lax.shift_right_arithmetic(number, 6).astype(jnp.float32),
                (number & 63).astype(jnp.float32),
            ]
            lefts.append(spread(parts, lax.shift_right_arithmetic(slot, 7), slot_rows))
            rights.append(
                jnp.where(matches(slot & (LANES - 1), LANES), 1.0, 0.0).astype(jnp.bfloat16)
            )
        found = found + contract(
            jnp.concatenate(lefts, axis=1), jnp.concatenate(rights, axis=1)
        )
    slot_idx[...] = (found[:slot_rows] * 64.0 + found[slot_rows:]).astype(jnp.int32) - 1

    for fill in fills[2:4]:
        fill.wait()

    def to_rows(table, source, rows):
        for c in range(3):
            for r in range(rows):
                table[c * rows + r : c * rows + r + 1, :] = source[
                    c : c + 1, r * LANES : (r + 1) * LANES
                ]

    to_rows(cur, disp, own_rows)
    lend_idx[...] = jnp.full_like(lend_idx, -1)
    for side in range(2):
        for r in range(lent_rows):
            at = side * lent_rows + r
            lend_idx[at : at + 1, :] = ghost[side : side + 1, r * LANES : (r + 1) * LANES]

    def box_copy(i, p, spot_out):
        return pltpu.make_async_remote_copy(
            src_ref=box_out.at[i, spot_out],
            dst_ref=box_in.at[i, me],
            send_sem=box_send.at[i],
            recv_sem=box_recv.at[i, kinds[p]],
            device_id=place_at(p),
            device_id_type=MESH,
        )

    def box_bytes(i, count, kind):
        every = pl.ds(0, count)
        return pltpu.make_async_remote_copy(
            src_ref=box_out.at[i, every],
            dst_ref=box_in.at[i, every],
            send_sem=box_send.at[i],
            recv_sem=box_recv.at[i, kind],
            device_id=place(lax.rem(me + 1, n)),
            device_id_type=MESH,
        )

    def box_start(i, spots, by_device):
        for p in spots:
            if p != my_p:
                box_copy(i, p, device_at(p) if by_device else p).start()

    def box_wait(i, kind):
        box_bytes(i, len([p for p in members[kind] if p != my_p]), kind).wait_recv()

    def halo_copies(i):
        copies = []
        for side, step in ((0, n - 1), (1, 1)):
            copies.append(
                pltpu.make_async_remote_copy(
                    src_ref=halo_out.at[i, side],
                    dst_ref=halo_in.at[i, 1 - side],
                    send_sem=halo_send.at[i, side],
                    recv_sem=halo_recv.at[i, 1 - side],
                    device_id=place(lax.rem(me + step, n)),
                    device_id_type=MESH,
                )
            )
        return copies

    def halo_start(i):
        for copy in halo_copies(i):
            copy.start()

    def halo_wait(i):
        for copy in halo_copies(i):
            copy.wait_recv()

    def halo_side(i, side, c):
        inside = me > 0 if side == 0 else me < n - 1
        return jnp.where(inside, halo_in[i, side, c : c + 1, :], 0.0)

    def box_row(i, devices):
        boxes = [box_in[i, device] for device in devices]
        return boxes[0] if per_row == 1 else jnp.concatenate(boxes, axis=1)

    def table_lines(table, rows, r):
        return [table[c * rows + r : c * rows + r + 1, :] for c in range(3)]

    for step in range(STEPS):
        going, back = 2 * step, 2 * step + 1

        def send_block(table, slots, j):
            row_of, lane_of = places_of(slots[j * SUBLANES : (j + 1) * SUBLANES, :])
            got = blank()
            for r in range(own_rows):
                pick(got, table_lines(table, own_rows, r), row_of, lane_of, r)
            spots = range(j * SUBLANES * per_row, (j + 1) * SUBLANES * per_row)
            for p in spots:
                r, l = divmod(p * cap - j * SUBLANES * LANES, LANES)
                for c in range(3):
                    box_out[going, p, c : c + 1, :] = got[c][r : r + 1, l : l + cap]
            if step == 0 and j == 0:
                pl.semaphore_wait(barrier, n - 1)
            box_start(going, spots, False)

        send_block(cur, slot_idx, 0)
        now_at = cur[...]
        slots = slot_idx[...]
        lent_at = places_of(lend_idx[...])
        for j in range(1, slot_rows // SUBLANES):
            send_block(now_at, slots, j)
        got = blank()
        for r in range(own_rows):
            pick(got, table_lines(now_at, own_rows, r), *lent_at, r)
        for c in range(3):
            for side in range(2):
                for r in range(lent_rows):
                    at = side * lent_rows + r
                    halo_out[going, side, c : c + 1, r * LANES : (r + 1) * LANES] = got[c][
                        at : at + 1
                    ]
        halo_start(going)
        box_in[going, me] = box_out[going, my_p]

        if step == 0:
            for fill in fills[4:]:
                fill.wait()

            @pl.loop(0, elnode)
            def _(k):
                set_row(k, conn[pl.ds(k, 1), :])

            for i in range(2):
                for r in range(pair_rows):
                    pair_idx[i * pair_rows + r : i * pair_rows + r + 1, :] = pair[
                        i : i + 1, r * LANES : (r + 1) * LANES
                    ]
            for i, first in ((0, near), (1, far)):
                for h in range(pair_groups):
                    set_row(first + h, pair[i : i + 1, h * width : (h + 1) * width])
            set_row(lend, flat_row(lend_idx, 0))
            to_rows(gaps, gap0, pair_rows)
            to_rows(slips, slip, pair_rows)
            to_rows(old, prev, own_rows)
            to_rows(loads, load, own_rows)
            mass[...] = 1.0 / mass[...]
            ue[...] = jnp.zeros_like(ue)
            stiff_parts[...] = jnp.zeros_like(stiff_parts)
            for c in range(3):
                for d in range(3):
                    block = stiff[c * elnode : (c + 1) * elnode, d * elnode : (d + 1) * elnode]
                    high, low = split(block)
                    for at, part in ((0, high), (1, high), (2, low)):
                        start = (3 * at + d) * wide
                        stiff_parts[c * wide : c * wide + elnode, start : start + elnode] = part

        def forces(cols):
            high, low = split(ue[:, cols])
            right = jnp.concatenate([high, low, high], axis=0).astype(jnp.bfloat16)
            left = stiff_parts[...].astype(jnp.bfloat16)
            product = jnp.dot(left, right, preferred_element_type=jnp.float32) * mod[:, cols]
            high, low = split(product)
            fe[0, :, cols] = high
            fe[1, :, cols] = low

        tops = [min(k, elnode - SUBLANES) for k in range(0, elnode, SUBLANES)]

        @pl.loop(0, chunks)
        def _(i):
            lanes = pl.ds(pl.multiple_of(i * LANES, LANES), LANES)
            for top in tops:
                row_of, lane_of = places_of(conn[top : top + SUBLANES, lanes])
                got = blank()
                for r in range(own_rows):
                    pick(got, table_lines(cur, own_rows, r), row_of, lane_of, r)
                for c in range(3):
                    ue[c * wide + top : c * wide + top + SUBLANES, lanes] = got[c]

        forces(slice(0, inner))

        pair_at = [places_of(pair_idx[i * pair_rows : (i + 1) * pair_rows, :]) for i in range(2)]
        ends = [blank(), blank()]

        def pair_pick(lines_of, row):
            for i in range(2):
                pick(ends[i], lines_of, *pair_at[i], row)

        def pair_picks(kind):
            box_wait(going, kind)
            for p in members[kind]:
                there = device_at(p)
                pair_pick([box_in[going, there, c : c + 1, :] for c in range(3)], there)

        if per_row == 1:
            for kind in range(KINDS - 1, 0, -1):
                pair_picks(kind)

        if per_row == 1:
            pair_picks(0)
        else:
            for kind in range(KINDS):
                box_wait(going, kind)
            for r in range(slot_rows):
                box = box_row(going, [r * per_row + t for t in range(per_row)])
                pair_pick([box[c : c + 1, :] for c in range(3)], r)
        gap = [
            gaps[c * pair_rows : (c + 1) * pair_rows, :] + ends[1][c] - ends[0][c] for c in range(3)
        ]
        normal = pen[...] * jnp.maximum(-gap[2], 0.0)
        length = jnp.sqrt(gap[0] * gap[0] + gap[1] * gap[1] + 0.01)
        slipping = slips[step * pair_rows : (step + 1) * pair_rows, :] == 1
        factor = jnp.where(slipping, -fric[...] * normal / length, -0.5 * pen[...])
        force = [factor * gap[0], factor * gap[1], normal]
        halves = [split(value) for value in force]
        total = jnp.zeros((6 * slot_rows, LANES), jnp.float32)
        for sign, first in ((1.0, far), (-1.0, near)):
            for h in range(pair_groups):
                parts = [
                    flat_row(sign * halves[c][s], h * chunks) for s in range(2) for c in range(3)
                ]
                k = first + h
                total = total + contract(
                    spread(parts, row_of_entry[k : k + 1, :], slot_rows), lane_hot[k]
                )
        total = total[: 3 * slot_rows] + total[3 * slot_rows :]
        for g in range(n):
            r, l = divmod(g * cap, LANES)
            for c in range(3):
                at = c * slot_rows + r
                box_out[back, g, c : c + 1, :] = total[at : at + 1, l : l + cap]
        box_start(back, range(n), True)
        box_in[back, me] = box_out[back, me]

        halo_wait(going)
        ghosts = [[halo_side(going, side, c) for c in range(3)] for side in range(2)]
        for top in tops:
            row_of, lane_of = places_of(conn[top : top + SUBLANES, inner:])
            for b in range((width - inner) // LANES):
                lanes = slice(b * LANES, (b + 1) * LANES)
                spots = slice(inner + b * LANES, inner + (b + 1) * LANES)
                got = [ue[c * wide + top : c * wide + top + SUBLANES, spots] for c in range(3)]
                for side in range(2):
                    for r in range(lent_rows):
                        lines = [
                            ghosts[side][c][:, r * LANES : (r + 1) * LANES] for c in range(3)
                        ]
                        at = own_rows + side * lent_rows + r
                        pick(got, lines, row_of[:, lanes], lane_of[:, lanes], at)
                for c in range(3):
                    ue[c * wide + top : c * wide + top + SUBLANES, spots] = got[c]
        forces(slice(inner, width))

        edge = jnp.zeros((6 * ghost_rows, LANES), jnp.float32)
        for first in range(0, elnode, chunks):
            lefts, rights = [], []
            for k in range(first, min(first + chunks, elnode)):
                row = row_of_entry[k : k + 1, inner:] - own_rows
                parts = [
                    fe[s, c * wide + k : c * wide + k + 1, inner:] for s in range(2) for c in range(3)
                ]
                lefts.append(spread(parts, row, ghost_rows))
                rights.append(lane_hot[k, :, inner:])
            edge = edge + contract(
                jnp.concatenate(lefts, axis=1), jnp.concatenate(rights, axis=1)
            )
        edge = edge[: 3 * ghost_rows] + edge[3 * ghost_rows :]
        for c in range(3):
            for side in range(2):
                for r in range(lent_rows):
                    at = c * ghost_rows + side * lent_rows + r
                    halo_out[back, side, c : c + 1, r * LANES : (r + 1) * LANES] = edge[at : at + 1]
        halo_start(back)

        if step == 0:
            for m in range(slot_groups):
                set_row(first_slot + m, flat_row(slot_idx, m * chunks))

        acc_e[...] = jnp.zeros_like(acc_e)
        some = next(f for f in (9, 3, 1) if elnode % f == 0)

        @pl.loop(0, elnode // some)
        def _(group):
            total = acc_e[...]
            for i in range(some):
                k = group * some + i
                parts = [
                    fe[s, pl.ds(c * wide + k, 1), :] for s in range(2) for c in range(3)
                ]
                total = total + contract(
                    spread(parts, row_of_entry[pl.ds(k, 1), :], own_rows), lane_hot[k]
                )
            acc_e[...] = total

        def home(rows):
            lefts, rights = [], []
            for at in range(0, len(rows), chunks):
                boxes, spots, hots = [], [], []
                for r in rows[at : at + chunks]:
                    k, l = first_slot + r // chunks, r % chunks * LANES
                    boxes.append(
                        box_row(back, [device_at(r * per_row + t) for t in range(per_row)])
                    )
                    spots.append(row_of_entry[k : k + 1, l : l + LANES])
                    hots.append(lane_hot[k, :, l : l + LANES])
                halves = split(jnp.concatenate(boxes, axis=1))
                parts = [halves[s][c : c + 1, :] for s in range(2) for c in range(3)]
                lefts.append(spread(parts, jnp.concatenate(spots, axis=1), own_rows))
                rights.append(jnp.concatenate(hots, axis=1))
            return lefts, rights

        def gathered(lefts, rights):
            return contract(jnp.concatenate(lefts, axis=1), jnp.concatenate(rights, axis=1))

        if per_row == 1:
            start = -(-members[1][0] // chunks) * chunks
            early, late = [*range(start, n), *range(members[1][0], start)], members[0]
        else:
            early, late = range(slot_rows - plane_rows, slot_rows), range(slot_rows - plane_rows)
            box_wait(back, 0)
        box_wait(back, 1)
        total = gathered(*home(early)) - acc_e[...]
        total = total[: 3 * own_rows] + total[3 * own_rows :]
        first_acc, first_u = [], []
        for c in range(3):
            rows = slice(c * own_rows, (c + 1) * own_rows)
            first_acc.append((loads[rows, :] + total[rows]) * mass[...])
            now = cur[rows, :]
            first_u.append(2.0 * now - old[rows, :] + time_step_sq * first_acc[c])
            if step < STEPS - 1:
                old[rows, :] = now
        if per_row == 1:
            box_wait(back, 0)
        halo_wait(back)
        lefts, rights = home(late)
        values = [
            jnp.concatenate([halo_side(back, 0, c), halo_side(back, 1, c)], axis=1)
            for c in range(3)
        ]
        halves = [split(-value) for value in values]
        parts = [halves[c][s] for s in range(2) for c in range(3)]
        lefts.append(spread(parts, row_of_entry[lend : lend + 1, :], own_rows))
        rights.append(lane_hot[lend])
        last = gathered(lefts, rights)
        last = last[: 3 * own_rows] + last[3 * own_rows :]
        for c in range(3):
            rows = slice(c * own_rows, (c + 1) * own_rows)
            change = last[rows] * mass[...]
            later = first_u[c] + time_step_sq * change
            if step == STEPS - 1:
                out_u[rows, :] = later
                out_a[rows, :] = first_acc[c] + change
            else:
                cur[rows, :] = later

    for i in range(2 * STEPS):
        box_bytes(i, n - 1, 0).wait_send()
        for copy in halo_copies(i):
            copy.wait_send()


def unflatten(rows, u, a, out_u, out_a):
    for table, out in ((u, out_u), (a, out_a)):
        for c in range(3):
            for r in range(rows):
                out[c : c + 1, r * LANES : (r + 1) * LANES] = table[c * rows + r : c * rows + r + 1, :]


def on_device(
    n_py,
    displacement,
    disp_prev,
    nodal_load,
    nodal_mass,
    modulus,
    stiffness,
    connectivity,
    ghost_send,
    contact_node,
    contact_owner,
    pair_ids,
    gap_start,
    penalty,
    friction,
    slip_state,
):
    n = lax.axis_size(("px", "py"))
    cap = 2 * contact_node.shape[0] // n
    elnode, width = connectivity.shape
    nodes = displacement.shape[1]
    lent = ghost_send.shape[1]
    own_rows = nodes // LANES
    slot_rows = n * cap // LANES
    wide = -(-elnode // SUBLANES) * SUBLANES
    pair_rows = pair_ids.shape[1] // LANES
    slot_groups = slot_rows * LANES // width
    pair_groups = pair_ids.shape[1] // width
    inner = width * 3 // 4
    entries = elnode + 1 + 2 * pair_groups + slot_groups
    flat = (3 * own_rows, LANES)
    vmem = pl.BlockSpec(memory_space=pltpu.VMEM)
    hbm = pl.BlockSpec(memory_space=pltpu.HBM)
    f32, bf16, i32 = jnp.float32, jnp.bfloat16, jnp.int32
    dma = pltpu.SemaphoreType.DMA
    args = [
        displacement,
        disp_prev,
        nodal_load,
        nodal_mass.reshape(-1, LANES),
        modulus.reshape(1, -1),
        stiffness,
        connectivity,
        ghost_send,
        contact_node.reshape(-1, LANES),
        contact_owner.reshape(-1, LANES),
        pair_ids,
        gap_start,
        penalty.reshape(-1, LANES),
        friction.reshape(-1, LANES),
        slip_state,
    ]
    new_u, acc = pl.pallas_call(
        functools.partial(kernel, (n_py, n, cap, elnode, lent, width, inner)),
        out_shape=[pltpu.VMEM(flat, f32)] * 2,
        in_specs=[hbm] * len(args),
        out_specs=[vmem] * 2,
        scratch_shapes=[pltpu.VMEM(a.shape, a.dtype) for a in args]
        + [
            pltpu.VMEM((entries, width), i32),
            pltpu.VMEM((entries, LANES, width), bf16),
            pltpu.VMEM((3 * wide, 9 * wide), f32),
            pltpu.VMEM((slot_rows, LANES), i32),
            pltpu.VMEM((2 * pair_rows, LANES), i32),
            pltpu.VMEM((SUBLANES, LANES), i32),
            pltpu.VMEM((3 * wide, width), f32),
            pltpu.VMEM((2, 3 * wide, width), f32),
            pltpu.VMEM((6 * own_rows, LANES), f32),
            pltpu.VMEM(flat, f32),
            pltpu.VMEM(flat, f32),
            pltpu.VMEM(flat, f32),
            pltpu.VMEM((3 * pair_rows, LANES), f32),
            pltpu.VMEM((3 * pair_rows, LANES), i32),
            pltpu.VMEM((2 * STEPS, n, 3, cap), f32),
            pltpu.VMEM((2 * STEPS, n, 3, cap), f32),
            pltpu.VMEM((2 * STEPS, 2, 3, lent), f32),
            pltpu.VMEM((2 * STEPS, 2, 3, lent), f32),
            dma((len(args),)),
            dma((2 * STEPS,)),
            dma((2 * STEPS, KINDS)),
            dma((2 * STEPS, 2)),
            dma((2 * STEPS, 2)),
        ],
        compiler_params=pltpu.CompilerParams(
            collective_id=0, has_side_effects=True, vmem_limit_bytes=66781184
        ),
        name="contact_steps",
    )(*args)
    return pl.pallas_call(
        functools.partial(unflatten, own_rows),
        out_shape=[jax.ShapeDtypeStruct(displacement.shape, f32)] * 2,
        in_specs=[vmem] * 2,
        out_specs=[vmem] * 2,
        compiler_params=pltpu.CompilerParams(vmem_limit_bytes=4 * 1024 * 1024),
        name="unflatten",
    )(new_u, acc)


def solution(mesh):
    both = ("px", "py")
    row, cols = P(both), P(None, both)
    return jax.shard_map(
        functools.partial(on_device, mesh.shape["py"]),
        mesh=mesh,
        in_specs=(cols, cols, cols, row, row, P(), cols, cols, row, row, cols, cols, row, row, cols),
        out_specs=(cols, cols),
        check_vma=False,
    )
```

```python
import functools

import jax
import jax.numpy as jnp
from jax import lax
from jax.experimental import pallas as pl
from jax.experimental.pallas import tpu as pltpu
from jax.sharding import PartitionSpec as P

STEPS = 3
LANES = 128
SUBLANES = 8
PLANES = 4
KINDS = 2
MESH = pl.DeviceIdType.MESH

time_step_sq = 0.05


def matches(index_row, rows):
    return lax.broadcasted_iota(jnp.int32, (rows, index_row.shape[1]), 0) == index_row


def split(value):
    high = value.astype(jnp.bfloat16).astype(jnp.float32)
    return high, value - high


def contract(left, right):
    return lax.dot_general(
        left, right, (((1,), (1,)), ((), ())), preferred_element_type=jnp.float32
    )


def spread(parts, row_index, rows):
    mask = matches(row_index, rows)
    return jnp.concatenate([jnp.where(mask, part, 0.0) for part in parts], axis=0).astype(
        jnp.bfloat16
    )


def pick(got, lines, row_of, lane_of, r):
    mask = row_of == r
    for c in range(3):
        line = jnp.broadcast_to(lines[c], (SUBLANES, LANES))
        value = jnp.take_along_axis(line, lane_of, axis=1, mode="promise_in_bounds")
        got[c] = jnp.where(mask, value, got[c])


def blank():
    return [jnp.zeros((SUBLANES, LANES), jnp.float32)] * 3


def places_of(index):
    return lax.shift_right_arithmetic(index, 7), index & (LANES - 1)


def kernel(
    dims,
    disp_hbm,
    prev_hbm,
    load_hbm,
    mass_hbm,
    mod_hbm,
    stiff_hbm,
    conn_hbm,
    ghost_hbm,
    node_hbm,
    owner_hbm,
    pair_hbm,
    gap_hbm,
    pen_hbm,
    fric_hbm,
    slip_hbm,
    out_u,
    out_a,
    disp,
    prev,
    load,
    mass,
    mod,
    stiff,
    conn,
    ghost,
    node,
    owner,
    pair,
    gap0,
    pen,
    fric,
    slip,
    row_of_entry,
    lane_hot,
    stiff_parts,
    slot_idx,
    pair_idx,
    lend_idx,
    ue,
    fe,
    acc_e,
    cur,
    old,
    loads,
    gaps,
    slips,
    box_out,
    box_in,
    halo_out,
    halo_in,
    in_sem,
    box_send,
    box_recv,
    halo_send,
    halo_recv,
):
    n_py, n, cap, elnode, lent, width, inner = dims
    px, py = lax.axis_index("px"), lax.axis_index("py")
    me = px * n_py + py

    def place(device):
        return {"px": lax.div(device, n_py), "py": lax.rem(device, n_py)}

    fills = [
        pltpu.make_async_copy(source, target, in_sem.at[i])
        for i, (source, target) in enumerate(
            [
                (owner_hbm, owner),
                (node_hbm, node),
                (disp_hbm, disp),
                (ghost_hbm, ghost),
                (conn_hbm, conn),
                (pair_hbm, pair),
                (stiff_hbm, stiff),
                (mod_hbm, mod),
                (gap_hbm, gap0),
                (slip_hbm, slip),
                (pen_hbm, pen),
                (fric_hbm, fric),
                (prev_hbm, prev),
                (load_hbm, load),
                (mass_hbm, mass),
            ]
        )
    ]
    per_plane = n // PLANES
    rows_y = n_py // PLANES
    rows_x = n // n_py // 2
    z, y = lax.div(py, rows_y), lax.rem(py, rows_y)
    x, core = lax.div(px, 2), lax.rem(px, 2)
    plane_at = [PLANES - 1 - z, lax.rem(z + 2, PLANES), z + 1 - 2 * lax.rem(z, 2), z]
    planes = [plane * rows_y for plane in plane_at]
    turns = [(a, e, b) for a in range(rows_x) for e in range(2) for b in range(rows_y)]
    columns = [
        (lax.rem(x + a, rows_x) * 2 + lax.rem(core + e, 2), lax.rem(y + b, rows_y))
        for a, e, b in turns
    ]

    def hops(place):
        j, (a, e, b) = place[0], turns[place[1]]
        return PLANES - 1 - j + min(a, rows_x - a) + min(b, rows_y - b) + 1 - e

    places = sorted(
        [(j, t) for j in range(PLANES) for t in range(per_plane)], key=hops, reverse=True
    )
    kinds = [0 if hops(place) > hops(places[0]) - 2 else 1 for place in places]
    my_p = places.index((PLANES - 1, 0))
    members = [[p for p in range(n) if kinds[p] == kind] for kind in range(KINDS)]

    def place_at(p):
        j, t = places[p]
        return {"px": columns[t][0], "py": columns[t][1] + planes[j]}

    def device_at(p):
        there = place_at(p)
        return there["px"] * n_py + there["py"]

    barrier = pltpu.get_barrier_semaphore()
    for p in range(n):
        if p != my_p:
            pl.semaphore_signal(barrier, inc=1, device_id=place_at(p), device_id_type=MESH)
    for fill in fills:
        fill.start()

    own_rows = cur.shape[0] // 3
    slot_rows = slot_idx.shape[0]
    plane_rows = slot_rows // PLANES
    per_row = LANES // cap
    wide = ue.shape[0] // 3
    lent_rows = lent // LANES
    ghost_rows = 2 * lent_rows
    chunks = width // LANES
    pair_rows = pair_idx.shape[0] // 2
    pair_groups = pair_rows // chunks
    slot_groups = slot_rows // chunks
    lend = elnode
    near, far = lend + 1, lend + 1 + pair_groups
    first_slot = far + pair_groups

    def set_row(k, row):
        row_of_entry[pl.ds(k, 1), :] = lax.shift_right_arithmetic(row, 7)
        lane_hot[k] = jnp.where(matches(row & (LANES - 1), LANES), 1.0, 0.0).astype(jnp.bfloat16)

    def flat_row(table, first):
        return jnp.concatenate([table[first + i : first + i + 1, :] for i in range(chunks)], axis=1)

    for fill in fills[:2]:
        fill.wait()

    from_lane = lax.broadcasted_iota(jnp.int32, (LANES, 2 * LANES), 0)
    to_lane = lax.broadcasted_iota(jnp.int32, (LANES, 2 * LANES), 1)
    before = jnp.where(from_lane < to_lane, 1.0, 0.0).astype(jnp.bfloat16)
    target = owner[...]
    target_py = lax.rem(target, n_py)
    target_z = lax.div(target_py, rows_y)
    target_j = jnp.where(
        target_z == plane_at[0],
        0,
        jnp.where(target_z == plane_at[1], 1, jnp.where(target_z == plane_at[2], 2, 3)),
    )
    target_px = lax.div(target, n_py)
    a = lax.rem(lax.div(target_px, 2) - x + rows_x, rows_x)
    e = lax.rem(lax.rem(target_px, 2) - core + 2, 2)
    b = lax.rem(lax.rem(target_py, rows_y) - y + rows_y, rows_y)
    turn = target_j * per_plane + (a * 2 + e) * rows_y + b
    spot = jnp.zeros_like(target)
    for p, (j, t) in enumerate(places):
        spot = jnp.where(turn == j * per_plane + t, p, spot)
    pieces = owner.shape[0]
    hot = [jnp.where(matches(spot[i : i + 1, :], n), 1.0, 0.0) for i in range(pieces)]
    counts = jnp.dot(
        jnp.concatenate(hot, axis=0).astype(jnp.bfloat16),
        before,
        preferred_element_type=jnp.float32,
    )
    carry = jnp.zeros((n, LANES), jnp.float32)
    ranks = []
    for i in range(pieces):
        earlier = counts[i * n : (i + 1) * n, :LANES]
        ranks.append(jnp.sum(hot[i] * (earlier + carry), axis=0, keepdims=True))
        carry = carry + counts[i * n : (i + 1) * n, LANES:]
    found = jnp.zeros((2 * slot_rows, LANES), jnp.float32)
    for first in range(0, pieces, chunks):
        lefts, rights = [], []
        for i in range(first, first + chunks):
            number = node[i : i + 1, :] + 1
            slot = spot[i : i + 1, :] * cap + ranks[i].astype(jnp.int32)
            parts = [
                lax.shift_right_arithmetic(number, 6).astype(jnp.float32),
                (number & 63).astype(jnp.float32),
            ]
            lefts.append(spread(parts, lax.shift_right_arithmetic(slot, 7), slot_rows))
            rights.append(
                jnp.where(matches(slot & (LANES - 1), LANES), 1.0, 0.0).astype(jnp.bfloat16)
            )
        found = found + contract(
            jnp.concatenate(lefts, axis=1), jnp.concatenate(rights, axis=1)
        )
    slot_idx[...] = (found[:slot_rows] * 64.0 + found[slot_rows:]).astype(jnp.int32) - 1

    for fill in fills[2:4]:
        fill.wait()

    def to_rows(table, source, rows):
        for c in range(3):
            for r in range(rows):
                table[c * rows + r : c * rows + r + 1, :] = source[
                    c : c + 1, r * LANES : (r + 1) * LANES
                ]

    to_rows(cur, disp, own_rows)
    lend_idx[...] = jnp.full_like(lend_idx, -1)
    for side in range(2):
        for r in range(lent_rows):
            at = side * lent_rows + r
            lend_idx[at : at + 1, :] = ghost[side : side + 1, r * LANES : (r + 1) * LANES]

    def box_copy(i, p, spot_out):
        return pltpu.make_async_remote_copy(
            src_ref=box_out.at[i, spot_out],
            dst_ref=box_in.at[i, me],
            send_sem=box_send.at[i],
            recv_sem=box_recv.at[i, kinds[p]],
            device_id=place_at(p),
            device_id_type=MESH,
        )

    def box_bytes(i, count, kind):
        every = pl.ds(0, count)
        return pltpu.make_async_remote_copy(
            src_ref=box_out.at[i, every],
            dst_ref=box_in.at[i, every],
            send_sem=box_send.at[i],
            recv_sem=box_recv.at[i, kind],
            device_id=place(lax.rem(me + 1, n)),
            device_id_type=MESH,
        )

    def box_start(i, spots, by_device):
        for p in spots:
            if p != my_p:
                box_copy(i, p, device_at(p) if by_device else p).start()

    def box_wait(i, kind):
        box_bytes(i, len([p for p in members[kind] if p != my_p]), kind).wait_recv()

    def halo_copies(i):
        copies = []
        for side, step in ((0, n - 1), (1, 1)):
            copies.append(
                pltpu.make_async_remote_copy(
                    src_ref=halo_out.at[i, side],
                    dst_ref=halo_in.at[i, 1 - side],
                    send_sem=halo_send.at[i, side],
                    recv_sem=halo_recv.at[i, 1 - side],
                    device_id=place(lax.rem(me + step, n)),
                    device_id_type=MESH,
                )
            )
        return copies

    def halo_start(i):
        for copy in halo_copies(i):
            copy.start()

    def halo_wait(i):
        for copy in halo_copies(i):
            copy.wait_recv()

    def halo_side(i, side, c):
        inside = me > 0 if side == 0 else me < n - 1
        return jnp.where(inside, halo_in[i, side, c : c + 1, :], 0.0)

    def box_row(i, devices):
        boxes = [box_in[i, device] for device in devices]
        return boxes[0] if per_row == 1 else jnp.concatenate(boxes, axis=1)

    def table_lines(table, rows, r):
        return [table[c * rows + r : c * rows + r + 1, :] for c in range(3)]

    for step in range(STEPS):
        going, back = 2 * step, 2 * step + 1

        def send_block(table, slots, j):
            row_of, lane_of = places_of(slots[j * SUBLANES : (j + 1) * SUBLANES, :])
            got = blank()
            for r in range(own_rows):
                pick(got, table_lines(table, own_rows, r), row_of, lane_of, r)
            spots = range(j * SUBLANES * per_row, (j + 1) * SUBLANES * per_row)
            for p in spots:
                r, l = divmod(p * cap - j * SUBLANES * LANES, LANES)
                for c in range(3):
                    box_out[going, p, c : c + 1, :] = got[c][r : r + 1, l : l + cap]
            if step == 0 and j == 0:
                pl.semaphore_wait(barrier, n - 1)
            box_start(going, spots, False)

        send_block(cur, slot_idx, 0)
        now_at = cur[...]
        slots = slot_idx[...]
        lent_at = places_of(lend_idx[...])
        for j in range(1, slot_rows // SUBLANES):
            send_block(now_at, slots, j)
        got = blank()
        for r in range(own_rows):
            pick(got, table_lines(now_at, own_rows, r), *lent_at, r)
        for c in range(3):
            for side in range(2):
                for r in range(lent_rows):
                    at = side * lent_rows + r
                    halo_out[going, side, c : c + 1, r * LANES : (r + 1) * LANES] = got[c][
                        at : at + 1
                    ]
        halo_start(going)
        box_in[going, me] = box_out[going, my_p]

        if step == 0:
            for fill in fills[4:]:
                fill.wait()

            @pl.loop(0, elnode)
            def _(k):
                set_row(k, conn[pl.ds(k, 1), :])

            for i in range(2):
                for r in range(pair_rows):
                    pair_idx[i * pair_rows + r : i * pair_rows + r + 1, :] = pair[
                        i : i + 1, r * LANES : (r + 1) * LANES
                    ]
            for i, first in ((0, near), (1, far)):
                for h in range(pair_groups):
                    set_row(first + h, pair[i : i + 1, h * width : (h + 1) * width])
            set_row(lend, flat_row(lend_idx, 0))
            to_rows(gaps, gap0, pair_rows)
            to_rows(slips, slip, pair_rows)
            to_rows(old, prev, own_rows)
            to_rows(loads, load, own_rows)
            mass[...] = 1.0 / mass[...]
            ue[...] = jnp.zeros_like(ue)
            stiff_parts[...] = jnp.zeros_like(stiff_parts)
            for c in range(3):
                for d in range(3):
                    block = stiff[c * elnode : (c + 1) * elnode, d * elnode : (d + 1) * elnode]
                    high, low = split(block)
                    for at, part in ((0, high), (1, high), (2, low)):
                        start = (3 * at + d) * wide
                        stiff_parts[c * wide : c * wide + elnode, start : start + elnode] = part

        def forces(cols):
            high, low = split(ue[:, cols])
            right = jnp.concatenate([high, low, high], axis=0).astype(jnp.bfloat16)
            left = stiff_parts[...].astype(jnp.bfloat16)
            product = jnp.dot(left, right, preferred_element_type=jnp.float32) * mod[:, cols]
            high, low = split(product)
            fe[0, :, cols] = high
            fe[1, :, cols] = low

        tops = [min(k, elnode - SUBLANES) for k in range(0, elnode, SUBLANES)]

        @pl.loop(0, chunks)
        def _(i):
            lanes = pl.ds(pl.multiple_of(i * LANES, LANES), LANES)
            for top in tops:
                row_of, lane_of = places_of(conn[top : top + SUBLANES, lanes])
                got = blank()
                for r in range(own_rows):
                    pick(got, table_lines(cur, own_rows, r), row_of, lane_of, r)
                for c in range(3):
                    ue[c * wide + top : c * wide + top + SUBLANES, lanes] = got[c]

        forces(slice(0, inner))

        pair_at = [places_of(pair_idx[i * pair_rows : (i + 1) * pair_rows, :]) for i in range(2)]
        ends = [blank(), blank()]

        def pair_pick(lines_of, row):
            for i in range(2):
                pick(ends[i], lines_of, *pair_at[i], row)

        def pair_picks(kind):
            box_wait(going, kind)
            for p in members[kind]:
                there = device_at(p)
                pair_pick([box_in[going, there, c : c + 1, :] for c in range(3)], there)

        if per_row == 1:
            for kind in range(KINDS - 1, 0, -1):
                pair_picks(kind)

        if per_row == 1:
            pair_picks(0)
        else:
            for kind in range(KINDS):
                box_wait(going, kind)
            for r in range(slot_rows):
                box = box_row(going, [r * per_row + t for t in range(per_row)])
                pair_pick([box[c : c + 1, :] for c in range(3)], r)
        gap = [
            gaps[c * pair_rows : (c + 1) * pair_rows, :] + ends[1][c] - ends[0][c] for c in range(3)
        ]
        normal = pen[...] * jnp.maximum(-gap[2], 0.0)
        length = jnp.sqrt(gap[0] * gap[0] + gap[1] * gap[1] + 0.01)
        slipping = slips[step * pair_rows : (step + 1) * pair_rows, :] == 1
        factor = jnp.where(slipping, -fric[...] * normal / length, -0.5 * pen[...])
        force = [factor * gap[0], factor * gap[1], normal]
        halves = [split(value) for value in force]
        total = jnp.zeros((6 * slot_rows, LANES), jnp.float32)
        for sign, first in ((1.0, far), (-1.0, near)):
            for h in range(pair_groups):
                parts = [
                    flat_row(sign * halves[c][s], h * chunks) for s in range(2) for c in range(3)
                ]
                k = first + h
                total = total + contract(
                    spread(parts, row_of_entry[k : k + 1, :], slot_rows), lane_hot[k]
                )
        total = total[: 3 * slot_rows] + total[3 * slot_rows :]
        for g in range(n):
            r, l = divmod(g * cap, LANES)
            for c in range(3):
                at = c * slot_rows + r
                box_out[back, g, c : c + 1, :] = total[at : at + 1, l : l + cap]
        box_start(back, range(n), True)
        box_in[back, me] = box_out[back, me]

        halo_wait(going)
        ghosts = [[halo_side(going, side, c) for c in range(3)] for side in range(2)]
        for top in tops:
            row_of, lane_of = places_of(conn[top : top + SUBLANES, inner:])
            for b in range((width - inner) // LANES):
                lanes = slice(b * LANES, (b + 1) * LANES)
                spots = slice(inner + b * LANES, inner + (b + 1) * LANES)
                got = [ue[c * wide + top : c * wide + top + SUBLANES, spots] for c in range(3)]
                for side in range(2):
                    for r in range(lent_rows):
                        lines = [
                            ghosts[side][c][:, r * LANES : (r + 1) * LANES] for c in range(3)
                        ]
                        at = own_rows + side * lent_rows + r
                        pick(got, lines, row_of[:, lanes], lane_of[:, lanes], at)
                for c in range(3):
                    ue[c * wide + top : c * wide + top + SUBLANES, spots] = got[c]
        forces(slice(inner, width))

        edge = jnp.zeros((6 * ghost_rows, LANES), jnp.float32)
        for first in range(0, elnode, chunks):
            lefts, rights = [], []
            for k in range(first, min(first + chunks, elnode)):
                row = row_of_entry[k : k + 1, inner:] - own_rows
                parts = [
                    fe[s, c * wide + k : c * wide + k + 1, inner:] for s in range(2) for c in range(3)
                ]
                lefts.append(spread(parts, row, ghost_rows))
                rights.append(lane_hot[k, :, inner:])
            edge = edge + contract(
                jnp.concatenate(lefts, axis=1), jnp.concatenate(rights, axis=1)
            )
        edge = edge[: 3 * ghost_rows] + edge[3 * ghost_rows :]
        for c in range(3):
            for side in range(2):
                for r in range(lent_rows):
                    at = c * ghost_rows + side * lent_rows + r
                    halo_out[back, side, c : c + 1, r * LANES : (r + 1) * LANES] = edge[at : at + 1]
        halo_start(back)

        if step == 0:
            for m in range(slot_groups):
                set_row(first_slot + m, flat_row(slot_idx, m * chunks))

        acc_e[...] = jnp.zeros_like(acc_e)
        some = next(f for f in (9, 3, 1) if elnode % f == 0)

        @pl.loop(0, elnode // some)
        def _(group):
            total = acc_e[...]
            for i in range(some):
                k = group * some + i
                parts = [
                    fe[s, pl.ds(c * wide + k, 1), :] for s in range(2) for c in range(3)
                ]
                total = total + contract(
                    spread(parts, row_of_entry[pl.ds(k, 1), :], own_rows), lane_hot[k]
                )
            acc_e[...] = total

        def home(rows):
            lefts, rights = [], []
            for at in range(0, len(rows), chunks):
                boxes, spots, hots = [], [], []
                for r in rows[at : at + chunks]:
                    k, l = first_slot + r // chunks, r % chunks * LANES
                    boxes.append(
                        box_row(back, [device_at(r * per_row + t) for t in range(per_row)])
                    )
                    spots.append(row_of_entry[k : k + 1, l : l + LANES])
                    hots.append(lane_hot[k, :, l : l + LANES])
                halves = split(jnp.concatenate(boxes, axis=1))
                parts = [halves[s][c : c + 1, :] for s in range(2) for c in range(3)]
                lefts.append(spread(parts, jnp.concatenate(spots, axis=1), own_rows))
                rights.append(jnp.concatenate(hots, axis=1))
            return lefts, rights

        def gathered(lefts, rights):
            return contract(jnp.concatenate(lefts, axis=1), jnp.concatenate(rights, axis=1))

        if per_row == 1:
            start = -(-members[1][0] // chunks) * chunks
            early, late = [*range(start, n), *range(members[1][0], start)], members[0]
        else:
            early, late = range(slot_rows - plane_rows, slot_rows), range(slot_rows - plane_rows)
            box_wait(back, 0)
        box_wait(back, 1)
        total = gathered(*home(early)) - acc_e[...]
        total = total[: 3 * own_rows] + total[3 * own_rows :]
        first_acc, first_u = [], []
        for c in range(3):
            rows = slice(c * own_rows, (c + 1) * own_rows)
            first_acc.append((loads[rows, :] + total[rows]) * mass[...])
            now = cur[rows, :]
            first_u.append(2.0 * now - old[rows, :] + time_step_sq * first_acc[c])
            if step < STEPS - 1:
                old[rows, :] = now
        if per_row == 1:
            box_wait(back, 0)
        halo_wait(back)
        lefts, rights = home(late)
        values = [
            jnp.concatenate([halo_side(back, 0, c), halo_side(back, 1, c)], axis=1)
            for c in range(3)
        ]
        halves = [split(-value) for value in values]
        parts = [halves[c][s] for s in range(2) for c in range(3)]
        lefts.append(spread(parts, row_of_entry[lend : lend + 1, :], own_rows))
        rights.append(lane_hot[lend])
        last = gathered(lefts, rights)
        last = last[: 3 * own_rows] + last[3 * own_rows :]
        for c in range(3):
            rows = slice(c * own_rows, (c + 1) * own_rows)
            change = last[rows] * mass[...]
            later = first_u[c] + time_step_sq * change
            if step == STEPS - 1:
                out_u[rows, :] = later
                out_a[rows, :] = first_acc[c] + change
            else:
                cur[rows, :] = later

    for i in range(2 * STEPS):
        box_bytes(i, n - 1, 0).wait_send()
        for copy in halo_copies(i):
            copy.wait_send()


def unflatten(rows, u, a, out_u, out_a):
    for table, out in ((u, out_u), (a, out_a)):
        for c in range(3):
            for r in range(rows):
                out[c : c + 1, r * LANES : (r + 1) * LANES] = table[c * rows + r : c * rows + r + 1, :]


def on_device(
    n_py,
    displacement,
    disp_prev,
    nodal_load,
    nodal_mass,
    modulus,
    stiffness,
    connectivity,
    ghost_send,
    contact_node,
    contact_owner,
    pair_ids,
    gap_start,
    penalty,
    friction,
    slip_state,
):
    n = lax.axis_size(("px", "py"))
    cap = 2 * contact_node.shape[0] // n
    elnode, width = connectivity.shape
    nodes = displacement.shape[1]
    lent = ghost_send.shape[1]
    own_rows = nodes // LANES
    slot_rows = n * cap // LANES
    wide = -(-elnode // SUBLANES) * SUBLANES
    pair_rows = pair_ids.shape[1] // LANES
    slot_groups = slot_rows * LANES // width
    pair_groups = pair_ids.shape[1] // width
    inner = width * 3 // 4
    entries = elnode + 1 + 2 * pair_groups + slot_groups
    flat = (3 * own_rows, LANES)
    vmem = pl.BlockSpec(memory_space=pltpu.VMEM)
    hbm = pl.BlockSpec(memory_space=pltpu.HBM)
    f32, bf16, i32 = jnp.float32, jnp.bfloat16, jnp.int32
    dma = pltpu.SemaphoreType.DMA
    args = [
        displacement,
        disp_prev,
        nodal_load,
        nodal_mass.reshape(-1, LANES),
        modulus.reshape(1, -1),
        stiffness,
        connectivity,
        ghost_send,
        contact_node.reshape(-1, LANES),
        contact_owner.reshape(-1, LANES),
        pair_ids,
        gap_start,
        penalty.reshape(-1, LANES),
        friction.reshape(-1, LANES),
        slip_state,
    ]
    new_u, acc = pl.pallas_call(
        functools.partial(kernel, (n_py, n, cap, elnode, lent, width, inner)),
        out_shape=[pltpu.VMEM(flat, f32)] * 2,
        in_specs=[hbm] * len(args),
        out_specs=[vmem] * 2,
        scratch_shapes=[pltpu.VMEM(a.shape, a.dtype) for a in args]
        + [
            pltpu.VMEM((entries, width), i32),
            pltpu.VMEM((entries, LANES, width), bf16),
            pltpu.VMEM((3 * wide, 9 * wide), f32),
            pltpu.VMEM((slot_rows, LANES), i32),
            pltpu.VMEM((2 * pair_rows, LANES), i32),
            pltpu.VMEM((SUBLANES, LANES), i32),
            pltpu.VMEM((3 * wide, width), f32),
            pltpu.VMEM((2, 3 * wide, width), f32),
            pltpu.VMEM((6 * own_rows, LANES), f32),
            pltpu.VMEM(flat, f32),
            pltpu.VMEM(flat, f32),
            pltpu.VMEM(flat, f32),
            pltpu.VMEM((3 * pair_rows, LANES), f32),
            pltpu.VMEM((3 * pair_rows, LANES), i32),
            pltpu.VMEM((2 * STEPS, n, 3, cap), f32),
            pltpu.VMEM((2 * STEPS, n, 3, cap), f32),
            pltpu.VMEM((2 * STEPS, 2, 3, lent), f32),
            pltpu.VMEM((2 * STEPS, 2, 3, lent), f32),
            dma((len(args),)),
            dma((2 * STEPS,)),
            dma((2 * STEPS, KINDS)),
            dma((2 * STEPS, 2)),
            dma((2 * STEPS, 2)),
        ],
        compiler_params=pltpu.CompilerParams(
            collective_id=0, has_side_effects=True, vmem_limit_bytes=66781184
        ),
        name="contact_steps",
    )(*args)
    return pl.pallas_call(
        functools.partial(unflatten, own_rows),
        out_shape=[jax.ShapeDtypeStruct(displacement.shape, f32)] * 2,
        in_specs=[vmem] * 2,
        out_specs=[vmem] * 2,
        compiler_params=pltpu.CompilerParams(vmem_limit_bytes=4 * 1024 * 1024),
        name="unflatten",
    )(new_u, acc)


def solution(mesh):
    both = ("px", "py")
    row, cols = P(both), P(None, both)
    return jax.shard_map(
        functools.partial(on_device, mesh.shape["py"]),
        mesh=mesh,
        in_specs=(cols, cols, cols, row, row, P(), cols, cols, row, row, cols, cols, row, row, cols),
        out_specs=(cols, cols),
        check_vma=False,
    )
```

```python
import functools

import jax
import jax.numpy as jnp
from jax import lax
from jax.experimental import pallas as pl
from jax.experimental.pallas import tpu as pltpu
from jax.sharding import PartitionSpec as P

STEPS = 3
LANES = 128
SUBLANES = 8
PLANES = 4
KINDS = 2
MESH = pl.DeviceIdType.MESH

time_step_sq = 0.05


def matches(index_row, rows):
    return lax.broadcasted_iota(jnp.int32, (rows, index_row.shape[1]), 0) == index_row


def split(value):
    high = value.astype(jnp.bfloat16).astype(jnp.float32)
    return high, value - high


def contract(left, right):
    return lax.dot_general(
        left, right, (((1,), (1,)), ((), ())), preferred_element_type=jnp.float32
    )


def spread(parts, row_index, rows):
    mask = matches(row_index, rows)
    return jnp.concatenate([jnp.where(mask, part, 0.0) for part in parts], axis=0).astype(
        jnp.bfloat16
    )


def pick(got, lines, row_of, lane_of, r):
    mask = row_of == r
    for c in range(3):
        line = jnp.broadcast_to(lines[c], (SUBLANES, LANES))
        value = jnp.take_along_axis(line, lane_of, axis=1, mode="promise_in_bounds")
        got[c] = jnp.where(mask, value, got[c])


def blank():
    return [jnp.zeros((SUBLANES, LANES), jnp.float32)] * 3


def places_of(index):
    return lax.shift_right_arithmetic(index, 7), index & (LANES - 1)


def kernel(
    dims,
    disp_hbm,
    prev_hbm,
    load_hbm,
    mass_hbm,
    mod_hbm,
    stiff_hbm,
    conn_hbm,
    ghost_hbm,
    node_hbm,
    owner_hbm,
    pair_hbm,
    gap_hbm,
    pen_hbm,
    fric_hbm,
    slip_hbm,
    out_u,
    out_a,
    disp,
    prev,
    load,
    mass,
    mod,
    stiff,
    conn,
    ghost,
    node,
    owner,
    pair,
    gap0,
    pen,
    fric,
    slip,
    row_of_entry,
    lane_hot,
    stiff_parts,
    slot_idx,
    pair_idx,
    lend_idx,
    ue,
    fe,
    acc_e,
    cur,
    old,
    loads,
    gaps,
    slips,
    box_out,
    box_in,
    halo_out,
    halo_in,
    in_sem,
    box_send,
    box_recv,
    halo_send,
    halo_recv,
):
    n_py, n, cap, elnode, lent, width, inner = dims
    px, py = lax.axis_index("px"), lax.axis_index("py")
    me = px * n_py + py

    def place(device):
        return {"px": lax.div(device, n_py), "py": lax.rem(device, n_py)}

    fills = [
        pltpu.make_async_copy(source, target, in_sem.at[i])
        for i, (source, target) in enumerate(
            [
                (owner_hbm, owner),
                (node_hbm, node),
                (disp_hbm, disp),
                (ghost_hbm, ghost),
                (conn_hbm, conn),
                (pair_hbm, pair),
                (stiff_hbm, stiff),
                (mod_hbm, mod),
                (gap_hbm, gap0),
                (slip_hbm, slip),
                (pen_hbm, pen),
                (fric_hbm, fric),
                (prev_hbm, prev),
                (load_hbm, load),
                (mass_hbm, mass),
            ]
        )
    ]
    per_plane = n // PLANES
    rows_y = n_py // PLANES
    rows_x = n // n_py // 2
    z, y = lax.div(py, rows_y), lax.rem(py, rows_y)
    x, core = lax.div(px, 2), lax.rem(px, 2)
    plane_at = [PLANES - 1 - z, lax.rem(z + 2, PLANES), z + 1 - 2 * lax.rem(z, 2), z]
    planes = [plane * rows_y for plane in plane_at]
    turns = [(a, e, b) for a in range(rows_x) for e in range(2) for b in range(rows_y)]
    columns = [
        (lax.rem(x + a, rows_x) * 2 + lax.rem(core + e, 2), lax.rem(y + b, rows_y))
        for a, e, b in turns
    ]

    def hops(place):
        j, (a, e, b) = place[0], turns[place[1]]
        return PLANES - 1 - j + min(a, rows_x - a) + min(b, rows_y - b) + 1 - e

    places = sorted(
        [(j, t) for j in range(PLANES) for t in range(per_plane)], key=hops, reverse=True
    )
    kinds = [0 if hops(place) > hops(places[0]) - 2 else 1 for place in places]
    my_p = places.index((PLANES - 1, 0))
    members = [[p for p in range(n) if kinds[p] == kind] for kind in range(KINDS)]

    def place_at(p):
        j, t = places[p]
        return {"px": columns[t][0], "py": columns[t][1] + planes[j]}

    def device_at(p):
        there = place_at(p)
        return there["px"] * n_py + there["py"]

    barrier = pltpu.get_barrier_semaphore()
    for p in range(n):
        if p != my_p:
            pl.semaphore_signal(barrier, inc=1, device_id=place_at(p), device_id_type=MESH)
    for fill in fills:
        fill.start()

    own_rows = cur.shape[0] // 3
    slot_rows = slot_idx.shape[0]
    plane_rows = slot_rows // PLANES
    per_row = LANES // cap
    wide = ue.shape[0] // 3
    lent_rows = lent // LANES
    ghost_rows = 2 * lent_rows
    chunks = width // LANES
    pair_rows = pair_idx.shape[0] // 2
    pair_groups = pair_rows // chunks
    slot_groups = slot_rows // chunks
    lend = elnode
    near, far = lend + 1, lend + 1 + pair_groups
    first_slot = far + pair_groups

    def set_row(k, row):
        row_of_entry[pl.ds(k, 1), :] = lax.shift_right_arithmetic(row, 7)
        lane_hot[k] = jnp.where(matches(row & (LANES - 1), LANES), 1.0, 0.0).astype(jnp.bfloat16)

    def flat_row(table, first):
        return jnp.concatenate([table[first + i : first + i + 1, :] for i in range(chunks)], axis=1)

    for fill in fills[:2]:
        fill.wait()

    from_lane = lax.broadcasted_iota(jnp.int32, (LANES, 2 * LANES), 0)
    to_lane = lax.broadcasted_iota(jnp.int32, (LANES, 2 * LANES), 1)
    before = jnp.where(from_lane < to_lane, 1.0, 0.0).astype(jnp.bfloat16)
    target = owner[...]
    target_py = lax.rem(target, n_py)
    target_z = lax.div(target_py, rows_y)
    target_j = jnp.where(
        target_z == plane_at[0],
        0,
        jnp.where(target_z == plane_at[1], 1, jnp.where(target_z == plane_at[2], 2, 3)),
    )
    target_px = lax.div(target, n_py)
    a = lax.rem(lax.div(target_px, 2) - x + rows_x, rows_x)
    e = lax.rem(lax.rem(target_px, 2) - core + 2, 2)
    b = lax.rem(lax.rem(target_py, rows_y) - y + rows_y, rows_y)
    turn = target_j * per_plane + (a * 2 + e) * rows_y + b
    spot = jnp.zeros_like(target)
    for p, (j, t) in enumerate(places):
        spot = jnp.where(turn == j * per_plane + t, p, spot)
    pieces = owner.shape[0]
    hot = [jnp.where(matches(spot[i : i + 1, :], n), 1.0, 0.0) for i in range(pieces)]
    counts = jnp.dot(
        jnp.concatenate(hot, axis=0).astype(jnp.bfloat16),
        before,
        preferred_element_type=jnp.float32,
    )
    carry = jnp.zeros((n, LANES), jnp.float32)
    ranks = []
    for i in range(pieces):
        earlier = counts[i * n : (i + 1) * n, :LANES]
        ranks.append(jnp.sum(hot[i] * (earlier + carry), axis=0, keepdims=True))
        carry = carry + counts[i * n : (i + 1) * n, LANES:]
    found = jnp.zeros((2 * slot_rows, LANES), jnp.float32)
    for first in range(0, pieces, chunks):
        lefts, rights = [], []
        for i in range(first, first + chunks):
            number = node[i : i + 1, :] + 1
            slot = spot[i : i + 1, :] * cap + ranks[i].astype(jnp.int32)
            parts = [
                lax.shift_right_arithmetic(number, 6).astype(jnp.float32),
                (number & 63).astype(jnp.float32),
            ]
            lefts.append(spread(parts, lax.shift_right_arithmetic(slot, 7), slot_rows))
            rights.append(
                jnp.where(matches(slot & (LANES - 1), LANES), 1.0, 0.0).astype(jnp.bfloat16)
            )
        found = found + contract(
            jnp.concatenate(lefts, axis=1), jnp.concatenate(rights, axis=1)
        )
    slot_idx[...] = (found[:slot_rows] * 64.0 + found[slot_rows:]).astype(jnp.int32) - 1

    for fill in fills[2:4]:
        fill.wait()

    def to_rows(table, source, rows):
        for c in range(3):
            for r in range(rows):
                table[c * rows + r : c * rows + r + 1, :] = source[
                    c : c + 1, r * LANES : (r + 1) * LANES
                ]

    to_rows(cur, disp, own_rows)
    lend_idx[...] = jnp.full_like(lend_idx, -1)
    for side in range(2):
        for r in range(lent_rows):
            at = side * lent_rows + r
            lend_idx[at : at + 1, :] = ghost[side : side + 1, r * LANES : (r + 1) * LANES]

    def box_copy(i, p, spot_out):
        return pltpu.make_async_remote_copy(
            src_ref=box_out.at[i, spot_out],
            dst_ref=box_in.at[i, me],
            send_sem=box_send.at[i],
            recv_sem=box_recv.at[i, kinds[p]],
            device_id=place_at(p),
            device_id_type=MESH,
        )

    def box_bytes(i, count, kind):
        every = pl.ds(0, count)
        return pltpu.make_async_remote_copy(
            src_ref=box_out.at[i, every],
            dst_ref=box_in.at[i, every],
            send_sem=box_send.at[i],
            recv_sem=box_recv.at[i, kind],
            device_id=place(lax.rem(me + 1, n)),
            device_id_type=MESH,
        )

    def box_start(i, spots, by_device):
        for p in spots:
            if p != my_p:
                box_copy(i, p, device_at(p) if by_device else p).start()

    def box_wait(i, kind):
        box_bytes(i, len([p for p in members[kind] if p != my_p]), kind).wait_recv()

    def halo_copies(i):
        copies = []
        for side, step in ((0, n - 1), (1, 1)):
            copies.append(
                pltpu.make_async_remote_copy(
                    src_ref=halo_out.at[i, side],
                    dst_ref=halo_in.at[i, 1 - side],
                    send_sem=halo_send.at[i, side],
                    recv_sem=halo_recv.at[i, 1 - side],
                    device_id=place(lax.rem(me + step, n)),
                    device_id_type=MESH,
                )
            )
        return copies

    def halo_start(i):
        for copy in halo_copies(i):
            copy.start()

    def halo_wait(i):
        for copy in halo_copies(i):
            copy.wait_recv()

    def halo_side(i, side, c):
        inside = me > 0 if side == 0 else me < n - 1
        return jnp.where(inside, halo_in[i, side, c : c + 1, :], 0.0)

    def box_row(i, devices):
        boxes = [box_in[i, device] for device in devices]
        return boxes[0] if per_row == 1 else jnp.concatenate(boxes, axis=1)

    def table_lines(table, rows, r):
        return [table[c * rows + r : c * rows + r + 1, :] for c in range(3)]

    for step in range(STEPS):
        going, back = 2 * step, 2 * step + 1

        def send_block(table, slots, j):
            row_of, lane_of = places_of(slots[j * SUBLANES : (j + 1) * SUBLANES, :])
            got = blank()
            for r in range(own_rows):
                pick(got, table_lines(table, own_rows, r), row_of, lane_of, r)
            spots = range(j * SUBLANES * per_row, (j + 1) * SUBLANES * per_row)
            for p in spots:
                r, l = divmod(p * cap - j * SUBLANES * LANES, LANES)
                for c in range(3):
                    box_out[going, p, c : c + 1, :] = got[c][r : r + 1, l : l + cap]
            if step == 0 and j == 0:
                pl.semaphore_wait(barrier, n - 1)
            box_start(going, spots, False)

        send_block(cur, slot_idx, 0)
        now_at = cur[...]
        slots = slot_idx[...]
        lent_at = places_of(lend_idx[...])
        for j in range(1, slot_rows // SUBLANES - 1):
            send_block(now_at, slots, j)
        got = blank()
        for r in range(own_rows):
            pick(got, table_lines(now_at, own_rows, r), *lent_at, r)
        for c in range(3):
            for side in range(2):
                for r in range(lent_rows):
                    at = side * lent_rows + r
                    halo_out[going, side, c : c + 1, r * LANES : (r + 1) * LANES] = got[c][
                        at : at + 1
                    ]
        halo_start(going)
        send_block(now_at, slots, slot_rows // SUBLANES - 1)
        box_in[going, me] = box_out[going, my_p]

        if step == 0:
            for fill in fills[4:]:
                fill.wait()

            @pl.loop(0, elnode)
            def _(k):
                set_row(k, conn[pl.ds(k, 1), :])

            for i in range(2):
                for r in range(pair_rows):
                    pair_idx[i * pair_rows + r : i * pair_rows + r + 1, :] = pair[
                        i : i + 1, r * LANES : (r + 1) * LANES
                    ]
            for i, first in ((0, near), (1, far)):
                for h in range(pair_groups):
                    set_row(first + h, pair[i : i + 1, h * width : (h + 1) * width])
            set_row(lend, flat_row(lend_idx, 0))
            to_rows(gaps, gap0, pair_rows)
            to_rows(slips, slip, pair_rows)
            to_rows(old, prev, own_rows)
            to_rows(loads, load, own_rows)
            mass[...] = 1.0 / mass[...]
            ue[...] = jnp.zeros_like(ue)
            stiff_parts[...] = jnp.zeros_like(stiff_parts)
            for c in range(3):
                for d in range(3):
                    block = stiff[c * elnode : (c + 1) * elnode, d * elnode : (d + 1) * elnode]
                    high, low = split(block)
                    for at, part in ((0, high), (1, high), (2, low)):
                        start = (3 * at + d) * wide
                        stiff_parts[c * wide : c * wide + elnode, start : start + elnode] = part

        def forces(cols):
            high, low = split(ue[:, cols])
            right = jnp.concatenate([high, low, high], axis=0).astype(jnp.bfloat16)
            left = stiff_parts[...].astype(jnp.bfloat16)
            product = jnp.dot(left, right, preferred_element_type=jnp.float32) * mod[:, cols]
            high, low = split(product)
            fe[0, :, cols] = high
            fe[1, :, cols] = low

        tops = [min(k, elnode - SUBLANES) for k in range(0, elnode, SUBLANES)]

        @pl.loop(0, chunks)
        def _(i):
            lanes = pl.ds(pl.multiple_of(i * LANES, LANES), LANES)
            for top in tops:
                row_of, lane_of = places_of(conn[top : top + SUBLANES, lanes])
                got = blank()
                for r in range(own_rows):
                    pick(got, table_lines(cur, own_rows, r), row_of, lane_of, r)
                for c in range(3):
                    ue[c * wide + top : c * wide + top + SUBLANES, lanes] = got[c]

        forces(slice(0, inner))

        pair_at = [places_of(pair_idx[i * pair_rows : (i + 1) * pair_rows, :]) for i in range(2)]
        ends = [blank(), blank()]

        def pair_pick(lines_of, row):
            for i in range(2):
                pick(ends[i], lines_of, *pair_at[i], row)

        def pair_picks(kind):
            for p in members[kind]:
                there = device_at(p)
                pair_pick([box_in[going, there, c : c + 1, :] for c in range(3)], there)

        if per_row == 1:
            box_wait(going, 1)
            pair_picks(1)

        if per_row > 1:
            box_wait(going, 1)
        box_wait(going, 0)
        halo_wait(going)
        if per_row == 1:
            pair_picks(0)
        else:
            for r in range(slot_rows):
                box = box_row(going, [r * per_row + t for t in range(per_row)])
                pair_pick([box[c : c + 1, :] for c in range(3)], r)
        ghosts = [[halo_side(going, side, c) for c in range(3)] for side in range(2)]
        for top in tops:
            row_of, lane_of = places_of(conn[top : top + SUBLANES, inner:])
            for b in range((width - inner) // LANES):
                lanes = slice(b * LANES, (b + 1) * LANES)
                spots = slice(inner + b * LANES, inner + (b + 1) * LANES)
                got = [ue[c * wide + top : c * wide + top + SUBLANES, spots] for c in range(3)]
                for side in range(2):
                    for r in range(lent_rows):
                        lines = [
                            ghosts[side][c][:, r * LANES : (r + 1) * LANES] for c in range(3)
                        ]
                        at = own_rows + side * lent_rows + r
                        pick(got, lines, row_of[:, lanes], lane_of[:, lanes], at)
                for c in range(3):
                    ue[c * wide + top : c * wide + top + SUBLANES, spots] = got[c]
        forces(slice(inner, width))

        gap = [
            gaps[c * pair_rows : (c + 1) * pair_rows, :] + ends[1][c] - ends[0][c] for c in range(3)
        ]
        normal = pen[...] * jnp.maximum(-gap[2], 0.0)
        length = jnp.sqrt(gap[0] * gap[0] + gap[1] * gap[1] + 0.01)
        slipping = slips[step * pair_rows : (step + 1) * pair_rows, :] == 1
        factor = jnp.where(slipping, -fric[...] * normal / length, -0.5 * pen[...])
        force = [factor * gap[0], factor * gap[1], normal]
        halves = [split(value) for value in force]
        total = jnp.zeros((6 * slot_rows, LANES), jnp.float32)
        for sign, first in ((1.0, far), (-1.0, near)):
            for h in range(pair_groups):
                parts = [
                    flat_row(sign * halves[c][s], h * chunks) for s in range(2) for c in range(3)
                ]
                k = first + h
                total = total + contract(
                    spread(parts, row_of_entry[k : k + 1, :], slot_rows), lane_hot[k]
                )
        total = total[: 3 * slot_rows] + total[3 * slot_rows :]
        for g in range(n):
            r, l = divmod(g * cap, LANES)
            for c in range(3):
                at = c * slot_rows + r
                box_out[back, g, c : c + 1, :] = total[at : at + 1, l : l + cap]
        box_start(back, range(n), True)
        box_in[back, me] = box_out[back, me]

        edge = jnp.zeros((6 * ghost_rows, LANES), jnp.float32)
        for first in range(0, elnode, chunks):
            lefts, rights = [], []
            for k in range(first, min(first + chunks, elnode)):
                row = row_of_entry[k : k + 1, inner:] - own_rows
                parts = [
                    fe[s, c * wide + k : c * wide + k + 1, inner:] for s in range(2) for c in range(3)
                ]
                lefts.append(spread(parts, row, ghost_rows))
                rights.append(lane_hot[k, :, inner:])
            edge = edge + contract(
                jnp.concatenate(lefts, axis=1), jnp.concatenate(rights, axis=1)
            )
        edge = edge[: 3 * ghost_rows] + edge[3 * ghost_rows :]
        for c in range(3):
            for side in range(2):
                for r in range(lent_rows):
                    at = c * ghost_rows + side * lent_rows + r
                    halo_out[back, side, c : c + 1, r * LANES : (r + 1) * LANES] = edge[at : at + 1]
        halo_start(back)

        if step == 0:
            for m in range(slot_groups):
                set_row(first_slot + m, flat_row(slot_idx, m * chunks))

        acc_e[...] = jnp.zeros_like(acc_e)
        some = next(f for f in (9, 3, 1) if elnode % f == 0)

        @pl.loop(0, elnode // some)
        def _(group):
            total = acc_e[...]
            for i in range(some):
                k = group * some + i
                parts = [
                    fe[s, pl.ds(c * wide + k, 1), :] for s in range(2) for c in range(3)
                ]
                total = total + contract(
                    spread(parts, row_of_entry[pl.ds(k, 1), :], own_rows), lane_hot[k]
                )
            acc_e[...] = total

        def home(rows):
            lefts, rights = [], []
            for at in range(0, len(rows), chunks):
                boxes, spots, hots = [], [], []
                for r in rows[at : at + chunks]:
                    k, l = first_slot + r // chunks, r % chunks * LANES
                    boxes.append(
                        box_row(back, [device_at(r * per_row + t) for t in range(per_row)])
                    )
                    spots.append(row_of_entry[k : k + 1, l : l + LANES])
                    hots.append(lane_hot[k, :, l : l + LANES])
                halves = split(jnp.concatenate(boxes, axis=1))
                parts = [halves[s][c : c + 1, :] for s in range(2) for c in range(3)]
                lefts.append(spread(parts, jnp.concatenate(spots, axis=1), own_rows))
                rights.append(jnp.concatenate(hots, axis=1))
            return lefts, rights

        def gathered(lefts, rights):
            return contract(jnp.concatenate(lefts, axis=1), jnp.concatenate(rights, axis=1))

        if per_row == 1:
            start = -(-members[1][0] // chunks) * chunks
            early, late = [*range(start, n), *range(members[1][0], start)], members[0]
        else:
            early, late = range(slot_rows - plane_rows, slot_rows), range(slot_rows - plane_rows)
            box_wait(back, 0)
        box_wait(back, 1)
        total = gathered(*home(early)) - acc_e[...]
        total = total[: 3 * own_rows] + total[3 * own_rows :]
        first_acc, first_u = [], []
        for c in range(3):
            rows = slice(c * own_rows, (c + 1) * own_rows)
            first_acc.append((loads[rows, :] + total[rows]) * mass[...])
            now = cur[rows, :]
            first_u.append(2.0 * now - old[rows, :] + time_step_sq * first_acc[c])
            if step < STEPS - 1:
                old[rows, :] = now
        if per_row == 1:
            box_wait(back, 0)
        halo_wait(back)
        lefts, rights = home(late)
        values = [
            jnp.concatenate([halo_side(back, 0, c), halo_side(back, 1, c)], axis=1)
            for c in range(3)
        ]
        halves = [split(-value) for value in values]
        parts = [halves[c][s] for s in range(2) for c in range(3)]
        lefts.append(spread(parts, row_of_entry[lend : lend + 1, :], own_rows))
        rights.append(lane_hot[lend])
        last = gathered(lefts, rights)
        last = last[: 3 * own_rows] + last[3 * own_rows :]
        for c in range(3):
            rows = slice(c * own_rows, (c + 1) * own_rows)
            change = last[rows] * mass[...]
            later = first_u[c] + time_step_sq * change
            if step == STEPS - 1:
                out_u[rows, :] = later
                out_a[rows, :] = first_acc[c] + change
            else:
                cur[rows, :] = later

    for i in range(2 * STEPS):
        box_bytes(i, n - 1, 0).wait_send()
        for copy in halo_copies(i):
            copy.wait_send()


def unflatten(rows, u, a, out_u, out_a):
    for table, out in ((u, out_u), (a, out_a)):
        for c in range(3):
            for r in range(rows):
                out[c : c + 1, r * LANES : (r + 1) * LANES] = table[c * rows + r : c * rows + r + 1, :]


def on_device(
    n_py,
    displacement,
    disp_prev,
    nodal_load,
    nodal_mass,
    modulus,
    stiffness,
    connectivity,
    ghost_send,
    contact_node,
    contact_owner,
    pair_ids,
    gap_start,
    penalty,
    friction,
    slip_state,
):
    n = lax.axis_size(("px", "py"))
    cap = 2 * contact_node.shape[0] // n
    elnode, width = connectivity.shape
    nodes = displacement.shape[1]
    lent = ghost_send.shape[1]
    own_rows = nodes // LANES
    slot_rows = n * cap // LANES
    wide = -(-elnode // SUBLANES) * SUBLANES
    pair_rows = pair_ids.shape[1] // LANES
    slot_groups = slot_rows * LANES // width
    pair_groups = pair_ids.shape[1] // width
    inner = width * 3 // 4
    entries = elnode + 1 + 2 * pair_groups + slot_groups
    flat = (3 * own_rows, LANES)
    vmem = pl.BlockSpec(memory_space=pltpu.VMEM)
    hbm = pl.BlockSpec(memory_space=pltpu.HBM)
    f32, bf16, i32 = jnp.float32, jnp.bfloat16, jnp.int32
    dma = pltpu.SemaphoreType.DMA
    args = [
        displacement,
        disp_prev,
        nodal_load,
        nodal_mass.reshape(-1, LANES),
        modulus.reshape(1, -1),
        stiffness,
        connectivity,
        ghost_send,
        contact_node.reshape(-1, LANES),
        contact_owner.reshape(-1, LANES),
        pair_ids,
        gap_start,
        penalty.reshape(-1, LANES),
        friction.reshape(-1, LANES),
        slip_state,
    ]
    new_u, acc = pl.pallas_call(
        functools.partial(kernel, (n_py, n, cap, elnode, lent, width, inner)),
        out_shape=[pltpu.VMEM(flat, f32)] * 2,
        in_specs=[hbm] * len(args),
        out_specs=[vmem] * 2,
        scratch_shapes=[pltpu.VMEM(a.shape, a.dtype) for a in args]
        + [
            pltpu.VMEM((entries, width), i32),
            pltpu.VMEM((entries, LANES, width), bf16),
            pltpu.VMEM((3 * wide, 9 * wide), f32),
            pltpu.VMEM((slot_rows, LANES), i32),
            pltpu.VMEM((2 * pair_rows, LANES), i32),
            pltpu.VMEM((SUBLANES, LANES), i32),
            pltpu.VMEM((3 * wide, width), f32),
            pltpu.VMEM((2, 3 * wide, width), f32),
            pltpu.VMEM((6 * own_rows, LANES), f32),
            pltpu.VMEM(flat, f32),
            pltpu.VMEM(flat, f32),
            pltpu.VMEM(flat, f32),
            pltpu.VMEM((3 * pair_rows, LANES), f32),
            pltpu.VMEM((3 * pair_rows, LANES), i32),
            pltpu.VMEM((2 * STEPS, n, 3, cap), f32),
            pltpu.VMEM((2 * STEPS, n, 3, cap), f32),
            pltpu.VMEM((2 * STEPS, 2, 3, lent), f32),
            pltpu.VMEM((2 * STEPS, 2, 3, lent), f32),
            dma((len(args),)),
            dma((2 * STEPS,)),
            dma((2 * STEPS, KINDS)),
            dma((2 * STEPS, 2)),
            dma((2 * STEPS, 2)),
        ],
        compiler_params=pltpu.CompilerParams(
            collective_id=0, has_side_effects=True, vmem_limit_bytes=66781184
        ),
        name="contact_steps",
    )(*args)
    return pl.pallas_call(
        functools.partial(unflatten, own_rows),
        out_shape=[jax.ShapeDtypeStruct(displacement.shape, f32)] * 2,
        in_specs=[vmem] * 2,
        out_specs=[vmem] * 2,
        compiler_params=pltpu.CompilerParams(vmem_limit_bytes=4 * 1024 * 1024),
        name="unflatten",
    )(new_u, acc)


def solution(mesh):
    both = ("px", "py")
    row, cols = P(both), P(None, both)
    return jax.shard_map(
        functools.partial(on_device, mesh.shape["py"]),
        mesh=mesh,
        in_specs=(cols, cols, cols, row, row, P(), cols, cols, row, row, cols, cols, row, row, cols),
        out_specs=(cols, cols),
        check_vma=False,
    )
```
